32 devices in a mesh: groups: 2 (over x), mix: 16 (over z, y, core).
Axes of the slice: x: 2, y: 2, z: 4, core: 2. Of those that a mesh axis runs over, the one named last changes fastest.
Arguments:
- resid_in: bfloat16 [4096, 2048], P(('groups', 'mix')), parts along dimension 0, may hold values from -40 to 40
- head_in: bfloat16 [4096, 4096], P('groups', 'mix'), parts along dimension 0, may hold values from -6 to 6
- gate_in: bfloat16 [4096, 4096], P('groups', 'mix'), parts along dimension 0, may hold values from -64 to 64
- in_basis: bfloat16 [4096, 128], P('groups'), parts along dimension 0, may hold values from -6 to 6
- out_basis: bfloat16 [4096, 128], P('groups'), parts along dimension 0, may hold values from -6 to 6
- step_size: float32 [64, 4096], P('mix', 'groups'), parts along dimension 1, may hold values from 0 to 2
- decay_rate: float32 [64], P('mix'), may hold values from 0.5 to 2
- init_state: float32 [16, 64, 64, 128], P('groups', 'mix'), parts along dimension 0, may hold values from -0.6 to 0.6
- lengths: int32 [16], P('groups'), parts along dimension 0, may hold values from 1 to 512, 2048 in all
- norm_gain: float32 [4096], replicated, may hold values from 0.1 to 1.9
- out_proj: bfloat16 [4096, 2048], P('mix'), may hold values from -0.09375 to 0.09375
- moe_gain: float32 [2048], replicated, may hold values from 0.1 to 1.9
- expert_ids: int32 [4096, 8], P(('groups', 'mix')), parts along dimension 0, may hold values from 0 to 31, as said below
- route_weight: float32 [4096, 8], P(('groups', 'mix')), parts along dimension 0, may hold values from 0.1 to 0.4
- placement: int32 [32], replicated, may hold values from 0 to 31, each once
- w_gate: bfloat16 [32, 2048, 768], P('mix'), may hold values from -0.125 to 0.125
- w_up: bfloat16 [32, 2048, 768], P('mix'), may hold values from -0.125 to 0.125
- w_down: bfloat16 [32, 768, 2048], P('mix'), may hold values from -0.21875 to 0.21875
Outputs:
- layer_out: bfloat16 [4096, 2048], P(('groups', 'mix')), parts along dimension 0
The draws below stay inside these ranges and needn't reach their ends.
There are 2 independent parts, one for each index of `groups`. The reference program is written for one: setup_inputs(seed, part) draws one part's arguments, and reference() takes and returns one part's arrays. A program takes and returns all parts, laid end to end along the dimension named above; an argument that names none is the same for every part. Nothing has to cross between parts.
Inputs may be any that keep to these rules, and one draw needn't show every extreme that they name: `expert_ids`: each row names 8 different experts. Within each aligned block of 128 rows (one device's rows), 8 experts appear exactly 64 times each, 8 others 64 / 2 times each and the rest 64 / 4 times each; each of the three sets is the same in every block. `placement`: each slot once. `lengths`: requests fill the 2048 positions in order.
All inputs are finite; a program needn't handle non-finite values.
Results may differ from the reference program's by a relative error of at most 0.013.
Values may be sent and summed in bfloat16 or wider, within the bound.
No kernel may reach another device: no remote copies, remote signals or barrier semaphores. Data moves between devices by JAX's collectives and lax.ppermute only.
A program may use at most 128 MiB of HBM per device.

```python
import math
import jax
import jax.numpy as jnp
import numpy as np
from jax import lax

D = 2048
HEADS = 64
HEAD_DIM = 64
STATE = 128
SPAN = 256
FFE = 768
TOPK = 8
REQUEST_COUNT = 8
TOK_DEV = 128
TOKEN_COUNT = 2048
EXPERTS = 32
MOST = 512
CAP = 64
N_MIX = 16


def draw_step_size(key, part):
    split_random_keys = jax.random.split(jax.random.fold_in(key, 11), 6)
    fast_heads = jax.random.uniform(split_random_keys[0], (HEADS,)) < 0.5
    fast_base = jax.random.uniform(split_random_keys[1], (HEADS,), minval=0.03, maxval=0.06)
    slow_base = jax.random.uniform(split_random_keys[2], (HEADS,), minval=0.1, maxval=0.3) / MOST
    baseline_rate = jnp.where(fast_heads, fast_base, slow_base)
    random_offset = jnp.exp(jax.random.uniform(split_random_keys[3], (HEADS, TOKEN_COUNT), minval=math.log(0.5), maxval=math.log(2.0)))
    spike_position = jax.random.randint(split_random_keys[4], (2 * REQUEST_COUNT,), 0, TOKEN_COUNT)
    spike_length = jax.random.uniform(split_random_keys[5], (2 * REQUEST_COUNT,), minval=0.25, maxval=0.5)
    spike_events = jnp.zeros((TOKEN_COUNT,), jnp.float32).at[spike_position].set(spike_length)
    return (baseline_rate[:, None] * random_offset + spike_events[None, :]).astype(jnp.float32)


def draw_gate_in(key, part):
    split_random_keys = jax.random.split(jax.random.fold_in(key, 23), 3)
    width_all = HEADS * HEAD_DIM
    head_share = (jnp.arange(width_all) // HEAD_DIM).astype(jnp.float32) / (HEADS - 1)
    row_scale = jnp.exp(jax.random.uniform(split_random_keys[0], (TOKEN_COUNT, 1), minval=math.log(0.3), maxval=math.log(3.0)))
    col_scale = jnp.exp(jax.random.uniform(split_random_keys[1], (1, width_all), minval=math.log(0.3), maxval=math.log(3.0)))
    trend = 3.0 ** (0.5 * head_share)
    noise = jax.random.truncated_normal(split_random_keys[2], -4.0, 4.0, (TOKEN_COUNT, width_all))
    return (noise * row_scale * col_scale * trend[None, :]).astype(jnp.bfloat16)


def draw_resid_in(key, part):
    split_random_keys = jax.random.split(jax.random.fold_in(key, 37), 3)
    row_scale = jnp.exp(jax.random.uniform(split_random_keys[0], (TOKEN_COUNT, 1), minval=math.log(0.3), maxval=math.log(3.0)))
    col_scale = jnp.exp(jax.random.uniform(split_random_keys[1], (1, D), minval=math.log(0.3), maxval=math.log(3.0)))
    noise = jax.random.truncated_normal(split_random_keys[2], -4.0, 4.0, (TOKEN_COUNT, D))
    return (noise * row_scale * col_scale).astype(jnp.bfloat16)


def draw_expert_ids(key, part):
    blocks_count = TOKEN_COUNT // TOK_DEV
    order_key, block_key = jax.random.split(jax.random.fold_in(key, 41))
    ranking = jax.random.permutation(order_key, jnp.arange(EXPERTS, dtype=jnp.int32))
    position = jnp.arange(EXPERTS, dtype=jnp.int32)
    level = jnp.where(position < EXPERTS // 4, 0, jnp.where(position < EXPERTS // 2, 1, 2)).astype(jnp.int32)
    per_level = jnp.where(level == 0, CAP, jnp.where(level == 1, CAP // 2, CAP // 4)).astype(jnp.int32)

    def one_block(block_seed):
        first_key, second_key, third_key = jax.random.split(block_seed, 3)
        jitter_rank = jax.random.randint(first_key, (EXPERTS,), 0, EXPERTS).astype(jnp.int32)
        score_value = (level * EXPERTS + jitter_rank) * EXPERTS + position
        within = jnp.argsort(score_value, stable=True)
        shuffled = ranking[within]
        mixing = jax.random.permutation(second_key, jnp.arange(EXPERTS, dtype=jnp.int32))
        labels = jnp.repeat(shuffled[mixing], per_level[mixing], total_repeat_length=TOK_DEV * TOPK)
        table = labels.reshape(TOPK, TOK_DEV).T
        row_order = jax.random.permutation(third_key, jnp.arange(TOK_DEV, dtype=jnp.int32))
        return table[row_order]
    block_seeds = jax.random.split(block_key, blocks_count)
    return jax.vmap(one_block)(block_seeds).reshape(TOKEN_COUNT, TOPK).astype(jnp.int32)


def levels(rng, extent, shards, smallest, high):
    def one(dim, shards_of):
        draws = jax.random.uniform(jax.random.fold_in(jax.random.fold_in(rng, 6), dim), (shards_of,), jnp.float32, smallest / len(shards), high / len(shards))
        return jnp.repeat(jnp.exp(draws), extent[dim] // shards_of).reshape((-1,) + (1,) * (len(extent) - dim - 1))

    gain = one(*shards[0])
    for cut in shards[1:]:
        gain = gain * one(*cut)
    return gain


def split_up(number_of, total, most, skew):
    portions = [(1 << 20) // math.isqrt(standing ** skew) + 1 for standing in range(2, number_of + 1)]
    rest, given = total - most - (number_of - 1), [1] * (number_of - 1)
    while rest > 0:
        candidates = [i for i in range(number_of - 1) if given[i] < most]
        mass, budget = sum([portions[i] for i in candidates]), rest
        for i in candidates:
            extra = min(most - given[i], max(1, budget * portions[i] // mass), rest)
            given[i] = given[i] + extra
            rest = rest - extra
    return np.array([most] + given)


def ragged(own_key, amount, total, bound, skew):
    if amount == 2:
        one = jax.random.randint(own_key, (), max(1, total - bound), min(bound, total - 1) + 1)
        return jnp.stack([one, total - one])
    sizes = jnp.asarray(split_up(amount, total, bound, skew), jnp.int32)
    couples = (amount - 1) // 2
    giver, sink = sizes[1:1 + 2 * couples:2], sizes[2:2 + 2 * couples:2]
    room = jnp.minimum(giver - 1, bound - sink)
    passed = jax.random.randint(jax.random.fold_in(own_key, 1), (couples,), 0, 1 << 20) % (room + 1)
    sizes = sizes.at[1:1 + 2 * couples:2].set(giver - passed).at[2:2 + 2 * couples:2].set(sink + passed)
    return sizes[jax.random.permutation(jax.random.fold_in(own_key, 2), amount)]


def bell_draw(key, dims, scale, bound, shards=(), held_as=jnp.bfloat16):
    drawn = scale * jax.random.normal(key, dims, jnp.float32)
    if shards:
        drawn = drawn * levels(key, dims, shards, -0.22, 0.18)
    return jnp.clip(drawn, -bound, bound).astype(held_as)


def setup_inputs(seed: int = 0, part: int = 0) -> dict:
    seeds = jax.random.split(jax.random.key(seed), 19)
    own_keys = jax.random.split(jax.random.fold_in(seeds[18], part), 19)
    return {
        "resid_in": draw_resid_in(jax.random.fold_in(jax.random.fold_in(seeds[18], part), 71), part),
        "head_in": bell_draw(own_keys[1], (TOKEN_COUNT, HEADS * HEAD_DIM), 1.0, 6.0, ((1, 16),)),
        "gate_in": draw_gate_in(jax.random.fold_in(jax.random.fold_in(seeds[18], part), 71), part),
        "in_basis": bell_draw(own_keys[3], (TOKEN_COUNT, STATE), 1.0, 6.0),
        "out_basis": bell_draw(own_keys[4], (TOKEN_COUNT, STATE), 1.0, 6.0),
        "step_size": draw_step_size(jax.random.fold_in(jax.random.fold_in(seeds[18], part), 71), part),
        "decay_rate": jnp.clip(jnp.exp(math.log(2.0) - 1.3862944 * jax.random.uniform(seeds[6], (HEADS,), jnp.float32) ** levels(seeds[6], (HEADS,), ((0, 16),), -0.2, 0.2)), 0.5, 2.0),
        "init_state": bell_draw(own_keys[7], (REQUEST_COUNT, HEADS, HEAD_DIM, STATE), 0.1, 0.6, ((1, 16),), jnp.float32),
        "lengths": ragged(own_keys[8], REQUEST_COUNT, TOKEN_COUNT, MOST, 2).astype(jnp.int32),
        "norm_gain": jnp.clip(1.0 + 0.18 * jax.random.normal(seeds[9], (HEADS * HEAD_DIM,), jnp.float32), 0.1, 1.9),
        "out_proj": bell_draw(seeds[10], (HEADS * HEAD_DIM, D), (HEADS * HEAD_DIM) ** -0.5, 0.09375, ((0, 16),)),
        "moe_gain": jnp.clip(1.0 + 0.18 * jax.random.normal(seeds[11], (D,), jnp.float32), 0.1, 1.9),
        "expert_ids": draw_expert_ids(jax.random.fold_in(jax.random.fold_in(seeds[18], part), 71), part),
        "route_weight": jnp.clip(0.1 + 0.3 * jax.random.uniform(own_keys[13], (TOKEN_COUNT, TOPK), jnp.float32) ** levels(own_keys[13], (TOKEN_COUNT, TOPK), ((0, 16),), -0.2, 0.2), 0.1, 0.4),
        "placement": jax.random.permutation(seeds[14], EXPERTS).astype(jnp.int32),
        "w_gate": bell_draw(seeds[15], (EXPERTS, D, FFE), D ** -0.5, 0.125, ((0, 16),)),
        "w_up": bell_draw(seeds[16], (EXPERTS, D, FFE), D ** -0.5, 0.125, ((0, 16),)),
        "w_down": bell_draw(seeds[17], (EXPERTS, FFE, D), FFE ** -0.5, 0.21875, ((0, 16),)),
    }


epsilon = 1e-05

def request_layout(lengths, tokens_total):
    request_end = jnp.cumsum(lengths).astype(jnp.int32)
    request_first = (request_end - lengths).astype(jnp.int32)
    position = jnp.arange(tokens_total, dtype=jnp.int32)
    segment = lax.optimization_barrier(jnp.sum((position[None, :] >= request_end[:, None]).astype(jnp.int32), axis=0)).astype(jnp.int32)
    member = segment[None, :] == jnp.arange(lengths.shape[0], dtype=jnp.int32)[:, None]
    first_of = lax.optimization_barrier(jnp.sum(jnp.where(member, request_first[:, None], 0), axis=0)).astype(jnp.int32)
    return (segment, first_of, member)

def scan_head(head_values, head_steps, head_rate, in_basis, out_basis, state_init, segment, first_of, member, block_len):
    tokens_total = head_values.shape[0]
    blocks = tokens_total // block_len
    highest = lax.Precision.HIGHEST
    log_decay = -head_steps * head_rate
    driven = head_values.astype(jnp.float32) * head_steps[:, None]

    def split_rows(array):
        return array.reshape((blocks, block_len) + array.shape[1:])
    block_first = jnp.arange(blocks, dtype=jnp.int32) * block_len
    member_blocks = member.reshape(member.shape[0], blocks, block_len).transpose(1, 0, 2)
    inputs = (split_rows(driven), split_rows(log_decay), split_rows(in_basis), split_rows(out_basis), split_rows(segment), split_rows(first_of), member_blocks, block_first)
    offsets = jnp.arange(block_len, dtype=jnp.int32)
    causal = offsets[None, :] <= offsets[:, None]

    def advance(state_in, block_in):
        drive_block, decay_block, basis_block, readout_block, segment_block, first_block, member_block, first_pos = block_in
        basis_wide = basis_block.astype(jnp.float32)
        readout_wide = readout_block.astype(jnp.float32)
        running = jnp.cumsum(decay_block)
        earlier = running - decay_block
        same_seq = (segment_block[:, None] == segment_block[None, :]) & causal
        gap_values = jnp.minimum(running[:, None] - running[None, :], 0.0)
        kernel = jnp.where(same_seq, jnp.exp(gap_values), 0.0)
        scores = jnp.dot(readout_block, basis_block.T, preferred_element_type=jnp.float32)
        output = jnp.dot(kernel * scores, drive_block, precision=highest)
        before = lax.optimization_barrier(jnp.max(jnp.where(same_seq, earlier[None, :], -jnp.inf), axis=1))
        carried = first_block < first_pos
        weight = jnp.exp(running - before)
        from_state = jnp.dot(readout_wide, state_in.T, precision=highest)
        projected = jnp.einsum('qn,rpn->rqp', readout_wide, state_init, precision=highest)
        from_init = lax.optimization_barrier(jnp.sum(member_block.astype(jnp.float32)[:, :, None] * projected, axis=0))
        output = output + weight[:, None] * jnp.where(carried[:, None], from_state, from_init)
        last_weight = jnp.where(same_seq[-1], jnp.exp(running[-1] - running), 0.0)
        state_out = jnp.dot((drive_block * last_weight[:, None]).T, basis_wide, precision=highest)
        init_last = jnp.einsum('r,rpn->pn', member_block[:, -1].astype(jnp.float32), state_init, precision=highest)
        source = jnp.where(carried[-1], state_in, init_last)
        state_out = state_out + weight[-1] * source
        return (state_out, output)
    empty_state = jnp.zeros((head_values.shape[1], in_basis.shape[1]), jnp.float32)
    _, outputs = lax.scan(advance, empty_state, inputs)
    return outputs.reshape(tokens_total, -1)

def reference(resid_in, head_in, gate_in, in_basis, out_basis, step_size, decay_rate, init_state, lengths, norm_gain, out_proj, moe_gain, expert_ids, route_weight, placement, w_gate, w_up, w_down):
    segment, first_of, member = request_layout(lengths, TOKEN_COUNT)
    head_inputs = head_in.reshape(TOKEN_COUNT, HEADS, HEAD_DIM).transpose(1, 0, 2)
    head_states = init_state.transpose(1, 0, 2, 3)

    def one_head(packed):
        head_values, head_steps, head_rate, state_init = packed
        return scan_head(head_values, head_steps, head_rate, in_basis, out_basis, state_init, segment, first_of, member, SPAN)
    head_outputs = lax.map(one_head, (head_inputs, step_size, decay_rate, head_states))
    scan_out = head_outputs.transpose(1, 0, 2).reshape(TOKEN_COUNT, HEADS * HEAD_DIM)
    gated_out = scan_out * jax.nn.silu(gate_in.astype(jnp.float32))
    squares = lax.optimization_barrier(jnp.sum(gated_out * gated_out, axis=1))
    mixed_in = (gated_out * norm_gain).astype(jnp.bfloat16)
    group_inputs = mixed_in.reshape(TOKEN_COUNT, N_MIX, -1).transpose(1, 0, 2)
    group_weights = out_proj.reshape(N_MIX, -1, D)

    def add_group(running_sum, packed):
        group_in, group_weight = packed
        group_term = jnp.dot(group_in, group_weight, preferred_element_type=jnp.float32).astype(jnp.bfloat16)
        group_term = lax.optimization_barrier(group_term)
        return (running_sum + group_term.astype(jnp.float32), None)
    mixer_sum, _ = lax.scan(add_group, jnp.zeros((TOKEN_COUNT, D), jnp.float32), (group_inputs, group_weights))
    mixer_out = mixer_sum * lax.rsqrt(squares / (HEADS * HEAD_DIM) + epsilon)[:, None]
    hidden = resid_in.astype(jnp.float32) + mixer_out
    normed = (hidden * lax.rsqrt(lax.optimization_barrier(jnp.mean(hidden * hidden, axis=1, keepdims=True)) + epsilon) * moe_gain).astype(jnp.bfloat16)
    flat_ids = expert_ids.reshape(-1).astype(jnp.int32)
    choose = (flat_ids[:, None] == jnp.arange(EXPERTS, dtype=jnp.int32)[None, :]).astype(jnp.int32)
    slot_rank = (lax.optimization_barrier(jnp.sum(jnp.cumsum(choose, axis=0) * choose, axis=1)) - 1).astype(jnp.int32)
    capacity = N_MIX * CAP
    token_of_pair = (jnp.arange(TOKEN_COUNT * TOPK, dtype=jnp.int32) // TOPK).astype(jnp.int32)
    token_table = jnp.zeros((EXPERTS, capacity), jnp.int32).at[flat_ids, slot_rank].set(token_of_pair)
    weight_table = jnp.zeros((EXPERTS, capacity), jnp.float32).at[flat_ids, slot_rank].set(route_weight.reshape(-1))

    def add_expert(expert_sum, expert):
        slot_index = placement[expert]
        picked_tokens = token_table[expert]
        chosen = jnp.take(normed, picked_tokens, axis=0)
        gate_part = jnp.dot(chosen, w_gate[slot_index], preferred_element_type=jnp.float32)
        up_part = jnp.dot(chosen, w_up[slot_index], preferred_element_type=jnp.float32)
        inner_act = (jax.nn.silu(gate_part) * up_part).astype(jnp.bfloat16)
        result = jnp.dot(inner_act, w_down[slot_index], preferred_element_type=jnp.float32).astype(jnp.bfloat16)
        result = lax.optimization_barrier(result)
        expert_sum = expert_sum.at[picked_tokens].add(weight_table[expert][:, None] * result.astype(jnp.float32))
        return (expert_sum, None)
    expert_sum, _ = lax.scan(add_expert, jnp.zeros((TOKEN_COUNT, D), jnp.float32), jnp.arange(EXPERTS, dtype=jnp.int32))
    return (hidden + expert_sum).astype(jnp.bfloat16)
```

```python
import functools

import jax
import jax.numpy as jnp
from jax import lax
from jax.experimental import pallas as pl
from jax.experimental.pallas import tpu as pltpu
from jax.sharding import PartitionSpec as P

HEADS = 64
HEAD_DIM = 64
epsilon = 1e-05
LANES = 128
NT = (((1,), (1,)), ((), ()))
TN = (((0,), (0,)), ((), ()))


def mm(a, b, dims=(((1,), (0,)), ((), ())), precision=None):
    return lax.dot_general(
        a, b, dims, precision=precision, preferred_element_type=jnp.float32
    )


def scan_kernel(
    starts, place, prep_ref, x_ref, g_ref, b_ref, c_ref, init_ref, out_ref, state, src, first_src,
    *, heads, requests
):
    span, width = x_ref.shape
    tok = out_ref.shape[3]
    head_dim = width // heads
    c0 = pl.program_id(0) * span
    steps = prep_ref[0:8, :]
    run = prep_ref[8:16, :]
    lane = lax.broadcasted_iota(jnp.int32, run.shape, 1)
    shift = 1
    while shift < span:
        run = run + jnp.where(lane >= shift, pltpu.roll(run, shift, 1), 0.0)
        shift *= 2
    before = jnp.zeros_like(run)
    first_last = jnp.int32(0)
    pos = lax.broadcasted_iota(jnp.int32, (span, 1), 0) + c0
    first = jnp.zeros_like(pos)
    inside = []
    for r in range(requests):
        start = starts[r]
        at = start - c0
        here = jnp.logical_and(at >= 0, at < span)
        inside.append(here)
        value = jnp.sum(jnp.where(lane == at - 1, run, 0.0), axis=1, keepdims=True)
        from_here = jnp.where(here, at, span)
        before = jnp.where(lane >= from_here, value, before)
        first_last = jnp.where(at < span, start, first_last)
        first = jnp.where(pos >= start, start, first)
    weight = jnp.exp(run - before)
    last = jnp.where(lane >= first_last - c0, jnp.exp(run[:, span - 1 : span] - run), 0.0)

    spread_row = lax.broadcasted_iota(jnp.int32, (8, width), 0)
    spread_col = lax.broadcasted_iota(jnp.int32, (8, width), 1) // head_dim
    spread = jnp.where(spread_row == spread_col, 1.0, 0.0)

    def widen(rows):
        return mm(rows, spread, TN, lax.Precision.HIGHEST)

    @pl.when(pl.program_id(0) == 0)
    def _():
        state[...] = jnp.zeros_like(state)

    drive = x_ref[...].astype(jnp.float32) * widen(steps)
    drive_low = drive.astype(jnp.bfloat16)
    drive_last = (drive * widen(last)).astype(jnp.bfloat16)
    basis = b_ref[...]
    readout = c_ref[...]
    row = lax.broadcasted_iota(jnp.int32, (span, span), 0)
    col = lax.broadcasted_iota(jnp.int32, (span, span), 1)
    valid = jnp.logical_and(col <= row, col >= first - c0)
    scores = jnp.where(valid, mm(readout, basis, NT), 0.0)

    src[...] = mm(readout, state[...].astype(jnp.bfloat16))
    first_src[...] = state[...]
    for r in range(requests):

        @pl.when(inside[r])
        def _(r=r):
            init = init_ref[r].T
            mine = mm(readout, init.astype(jnp.bfloat16))
            src[...] = jnp.where(first == starts[r], mine, src[...])
            first_src[...] = init

    weight_wide = widen(weight)
    run_cols = run.T
    per_tile = LANES // head_dim
    tile_lane = lax.broadcasted_iota(jnp.int32, (span, LANES), 1) // head_dim
    pieces = []
    for tile in range(heads // per_tile):
        drive_tile = drive_low[:, tile * LANES : (tile + 1) * LANES]
        piece = None
        for j in range(per_tile):
            h = tile * per_tile + j
            gap = jnp.minimum(run_cols[:, h : h + 1] - run[h : h + 1, :], 0.0)
            part = mm((jnp.exp(gap) * scores).astype(jnp.bfloat16), drive_tile)
            piece = part if piece is None else jnp.where(tile_lane == j, part, piece)
        pieces.append(piece)
    inner = pieces[0] if len(pieces) == 1 else jnp.concatenate(pieces, axis=1)
    output = inner + weight_wide * src[...]
    state[...] = mm(basis, drive_last, TN) + weight_wide[span - 1 : span, :] * first_src[...]
    gate = g_ref[...].astype(jnp.float32)
    gated = (output * (gate / (1.0 + jnp.exp(-gate)))).astype(jnp.bfloat16)
    for half in range(span // tok):
        out_ref[0, half ^ place[2], 0] = gated[half * tok : (half + 1) * tok]


def scan_heads(head_in, gate_in, in_basis, out_basis, step, rate, init, lengths, place, depth):
    tokens, width = head_in.shape
    heads = step.shape[0]
    requests = lengths.shape[0]
    states = in_basis.shape[1]
    tok = tokens // (4 * depth)
    span = 2 * tok
    ends = jnp.cumsum(lengths)
    starts = (ends - lengths).astype(jnp.int32)
    pad = ((0, 8 - heads), (0, 0))
    prep = jnp.concatenate([jnp.pad(step, pad), jnp.pad(-step * rate[:, None], pad)], axis=0)
    init = init.reshape(requests, width, states)
    cost = pl.CostEstimate(
        flops=2 * tokens * width * (span * 2 + 3 * states),
        bytes_accessed=6 * tokens * width,
        transcendentals=tokens * span * heads,
    )

    def row_block(i, starts, place):
        return (i, 0)

    def out_block(i, starts, place):
        return (place[1] ^ lax.rem(i, 2), 0, lax.rem(place[0] - lax.div(i, 2) + depth, depth), 0, 0)

    return pl.pallas_call(
        functools.partial(scan_kernel, heads=heads, requests=requests),
        out_shape=jax.ShapeDtypeStruct((2, 2, depth, tok, width), jnp.bfloat16),
        grid_spec=pltpu.PrefetchScalarGridSpec(
            num_scalar_prefetch=2,
            grid=(tokens // span,),
            in_specs=[
                pl.BlockSpec((16, span), lambda i, starts, place: (0, i)),
                pl.BlockSpec((span, width), row_block),
                pl.BlockSpec((span, width), row_block),
                pl.BlockSpec((span, states), row_block),
                pl.BlockSpec((span, states), row_block),
                pl.BlockSpec((requests, width, states), lambda i, starts, place: (0, 0, 0)),
            ],
            out_specs=pl.BlockSpec((1, 2, 1, tok, width), out_block),
            scratch_shapes=[
                pltpu.VMEM((states, width), jnp.float32),
                pltpu.VMEM((span, width), jnp.float32),
                pltpu.VMEM((states, width), jnp.float32),
            ],
        ),
        cost_estimate=cost,
        name="scan",
    )(starts, place, prep, head_in, gate_in, in_basis, out_basis, init)


def project_kernel(*refs):
    acts, weights, out_ref, squares_ref = refs[:4], refs[4:8], refs[8], refs[9]
    depth, tok, width = acts[0].shape
    total = None
    squares = jnp.zeros((depth * tok, 1), jnp.float32)
    for act, weight in zip(acts, weights):
        rows = act[...].reshape(depth * tok, width)
        part = mm(rows, weight[...])
        total = part if total is None else total + part
        wide = rows.astype(jnp.float32)
        squares = squares + jnp.sum(wide * wide, axis=1, keepdims=True)
    out_ref[...] = total.reshape(out_ref.shape).astype(jnp.bfloat16)
    squares_ref[...] = jnp.broadcast_to(squares, (depth * tok, LANES)).reshape(squares_ref.shape)


def project(acts, weights, columns):
    depth, tok, width = acts[0].shape
    model = weights[0].shape[1]
    steps = model // columns
    cost = pl.CostEstimate(
        flops=8 * depth * tok * width * model,
        bytes_accessed=2 * (4 * width * model + depth * tok * (model + 4 * width)),
        transcendentals=0,
    )
    return pl.pallas_call(
        project_kernel,
        out_shape=(
            jax.ShapeDtypeStruct((depth, tok, model), jnp.bfloat16),
            jax.ShapeDtypeStruct((depth, tok, LANES), jnp.float32),
        ),
        grid=(steps,),
        in_specs=[pl.BlockSpec((depth, tok, width), lambda i: (0, 0, 0))] * 4
        + [pl.BlockSpec((width, columns), lambda i: (0, i))] * 4,
        out_specs=(
            pl.BlockSpec((depth, tok, columns), lambda i: (0, 0, i)),
            pl.BlockSpec((depth, tok, LANES), lambda i: (0, 0, 0)),
        ),
        cost_estimate=cost,
        name="project",
    )(*acts, *weights)


def expert_kernel(place, *refs, blocks, cap, slots):
    x_refs = refs[:blocks]
    gate_ref, up_ref, down_ref = refs[blocks : blocks + 3]
    outs = refs[blocks + 3 : 2 * blocks + 3]
    rows, total, result = refs[2 * blocks + 3 :]
    expert, part = pl.program_id(0), pl.program_id(1)
    tok, model = outs[0].shape
    here = place[3] * pl.num_programs(0) + expert

    @pl.when(part == 0)
    def _():
        source = lax.broadcasted_iota(jnp.int32, (8, LANES), 1)
        pick = jnp.where(jnp.logical_or(source == here, source == here + slots), 1.0, 0.0)
        pick = pick.astype(jnp.bfloat16)
        above = lax.broadcasted_iota(jnp.int32, (tok, tok), 0)
        across = lax.broadcasted_iota(jnp.int32, (tok, tok), 1)
        earlier = jnp.where(above < across, 1.0, 0.0).astype(jnp.bfloat16)
        slot = lax.broadcasted_iota(jnp.int32, (cap, tok), 0)
        for b in range(blocks):
            weight = mm(pick, x_refs[b][:, model : model + LANES], NT)
            chosen = weight > 0.0
            rank = mm(jnp.where(chosen, 1.0, 0.0).astype(jnp.bfloat16), earlier)
            rank = jnp.where(chosen, rank, -1.0)[0:1, :].astype(jnp.int32)
            select = jnp.where(slot == rank, 1.0, 0.0).astype(jnp.bfloat16)
            picked = mm(select, x_refs[b][:, :model])
            rows[b * cap : (b + 1) * cap, :] = picked.astype(jnp.bfloat16)

    x = rows[...]
    gate = mm(x, gate_ref[0])
    up = mm(x, up_ref[0])
    act = (gate / (1.0 + jnp.exp(-gate)) * up).astype(jnp.bfloat16)
    down = mm(act, down_ref[0])

    @pl.when(part == 0)
    def _():
        total[...] = down

    @pl.when(part > 0)
    def _():
        total[...] += down

    @pl.when(part == pl.num_programs(1) - 1)
    def _():
        source = lax.broadcasted_iota(jnp.int32, (tok, LANES), 1)
        picks = jnp.logical_or(source == here, source == here + slots)
        below = lax.broadcasted_iota(jnp.int32, (tok, tok), 0)
        across = lax.broadcasted_iota(jnp.int32, (tok, tok), 1)
        earlier = jnp.where(across < below, 1.0, 0.0).astype(jnp.bfloat16)
        slot = lax.broadcasted_iota(jnp.int32, (tok, cap), 1)
        for b in range(blocks):
            table = x_refs[b][:, model : model + LANES].astype(jnp.float32)
            weight = jnp.sum(jnp.where(picks, table, 0.0), axis=1, keepdims=True)
            chosen = weight > 0.0
            marks = jnp.broadcast_to(jnp.where(chosen, 1.0, 0.0), (tok, LANES))
            rank = mm(earlier, marks.astype(jnp.bfloat16))[:, 0:1]
            rank = jnp.where(chosen, rank, -1.0).astype(jnp.int32)
            select = jnp.where(slot == rank, 1.0, 0.0).astype(jnp.bfloat16)
            value = weight * mm(select, total[b * cap : (b + 1) * cap, :].astype(jnp.bfloat16))

            @pl.when(expert == 0)
            def _():
                result[b] = value

            @pl.when(expert > 0)
            def _():
                result[b] += value

            @pl.when(expert == pl.num_programs(0) - 1)
            def _():
                outs[b][...] = result[b].astype(jnp.bfloat16)


def run_experts(xs, w_gate, w_up, w_down, place, cap, slots, parts):
    blocks = len(xs)
    tok, extended = xs[0].shape
    count, model, hidden = w_gate.shape
    tile = hidden // parts
    cost = pl.CostEstimate(
        flops=6 * count * blocks * cap * model * hidden,
        bytes_accessed=6 * count * model * hidden + 4 * blocks * tok * model,
        transcendentals=count * blocks * cap * hidden,
    )
    return pl.pallas_call(
        functools.partial(expert_kernel, blocks=blocks, cap=cap, slots=slots),
        out_shape=[jax.ShapeDtypeStruct((tok, model), jnp.bfloat16)] * blocks,
        grid_spec=pltpu.PrefetchScalarGridSpec(
            num_scalar_prefetch=1,
            grid=(count, parts),
            in_specs=[pl.BlockSpec((tok, extended), lambda e, f, place: (0, 0))] * blocks
            + [
                pl.BlockSpec((1, model, tile), lambda e, f, place: (e, 0, f)),
                pl.BlockSpec((1, model, tile), lambda e, f, place: (e, 0, f)),
                pl.BlockSpec((1, tile, model), lambda e, f, place: (e, f, 0)),
            ],
            out_specs=[pl.BlockSpec((tok, model), lambda e, f, place: (0, 0))] * blocks,
            scratch_shapes=[
                pltpu.VMEM((blocks * cap, model), jnp.bfloat16),
                pltpu.VMEM((blocks * cap, model), jnp.float32),
                pltpu.VMEM((blocks, tok, model), jnp.float32),
            ],
        ),
        compiler_params=pltpu.CompilerParams(vmem_limit_bytes=40 * 1024 * 1024),
        cost_estimate=cost,
        name="experts",
    )(place, *xs, w_gate, w_up, w_down)


def add_low(a, b):
    return (a.astype(jnp.float32) + b.astype(jnp.float32)).astype(jnp.bfloat16)


def local(
    resid_in, head_in, gate_in, in_basis, out_basis, step_size, decay_rate, init_state, lengths,
    norm_gain, out_proj, moe_gain, expert_ids, route_weight, placement, w_gate, w_up, w_down,
):
    devices = lax.axis_size("mix")
    depth = devices // 4
    me = lax.axis_index("mix")
    place = jnp.stack([me // 4, (me // 2) % 2, me % 2, me]).astype(jnp.int32)
    tokens = head_in.shape[0]
    tok = tokens // devices
    width = head_in.shape[1]
    model = out_proj.shape[1]

    def cross(x, mask):
        return lax.ppermute(x, "mix", [(i, i ^ mask) for i in range(devices)])

    def onward(x):
        return lax.ppermute(x, "mix", [(i, (i + 4) % devices) for i in range(devices)])

    gain = lax.dynamic_slice(norm_gain, (me * width,), (width,))
    proj = (out_proj.astype(jnp.float32) * gain[:, None]).astype(jnp.bfloat16)
    proj_y = cross(proj, 2)
    projs = [proj, cross(proj, 1), proj_y, cross(proj_y, 1)]

    slots = placement.shape[0]
    slot_of = jnp.sum(
        jnp.where(
            expert_ids[:, :, None] == jnp.arange(slots, dtype=jnp.int32), placement[None, None, :], 0
        ),
        axis=2,
    )
    route = jnp.sum(
        jnp.where(
            slot_of[:, :, None] == jnp.arange(slots, dtype=jnp.int32), route_weight[:, :, None], 0.0
        ),
        axis=1,
    )
    route_high = lax.reduce_precision(route, 8, 7)
    table = jnp.concatenate([route_high, route - route_high], axis=1)
    table = jnp.pad(table, ((0, 0), (0, LANES - 2 * slots))).astype(jnp.bfloat16)

    gated = scan_heads(
        head_in, gate_in, in_basis, out_basis, step_size, decay_rate, init_state, lengths, place, depth
    )
    acts = [gated[0, 0], cross(gated[0, 1], 1), cross(gated[1, 0], 2), cross(gated[1, 1], 3)]
    mixed, squares = project(acts, projs, 512)
    total, norm = mixed[1], squares[1, :, 0:1]
    for dz in range(2, depth):
        total = add_low(onward(total), mixed[dz])
        norm = onward(norm) + squares[dz, :, 0:1]
    mixer_sum = onward(total).astype(jnp.float32) + mixed[0].astype(jnp.float32)
    norm = onward(norm) + squares[0, :, 0:1]
    hidden = resid_in.astype(jnp.float32) + mixer_sum * lax.rsqrt(norm / (devices * width) + epsilon)
    normed = (
        hidden * lax.rsqrt(jnp.mean(hidden * hidden, axis=1, keepdims=True) + epsilon) * moe_gain
    ).astype(jnp.bfloat16)
    mine = jnp.concatenate([normed, table], axis=1)

    cap = 2 * tok * expert_ids.shape[1] // slots
    sums = []
    for dz in range(depth):
        if dz > 0:
            mine = onward(mine)
        other = cross(mine, 2)
        outs = run_experts(
            [mine, cross(mine, 1), other, cross(other, 1)],
            w_gate, w_up, w_down, place, cap, slots, 3,
        )
        near = add_low(outs[0], cross(outs[1], 1))
        far = add_low(outs[2], cross(outs[3], 1))
        sums.append(add_low(near, cross(far, 2)))
    total = sums[1]
    for dz in range(2, depth):
        total = add_low(onward(total), sums[dz])
    expert_sum = onward(total).astype(jnp.float32) + sums[0].astype(jnp.float32)
    return (hidden + expert_sum).astype(jnp.bfloat16)


def solution(mesh):
    return jax.shard_map(
        local,
        mesh=mesh,
        in_specs=(
            P(("groups", "mix"), None),
            P("groups", "mix"),
            P("groups", "mix"),
            P("groups", None),
            P("groups", None),
            P("mix", "groups"),
            P("mix"),
            P("groups", "mix", None, None),
            P("groups"),
            P(),
            P("mix", None),
            P(),
            P(("groups", "mix"), None),
            P(("groups", "mix"), None),
            P(),
            P("mix", None, None),
            P("mix", None, None),
            P("mix", None, None),
        ),
        out_specs=P(("groups", "mix"), None),
        check_vma=False,
    )
```

```python
import functools

import jax
import jax.numpy as jnp
from jax import lax
from jax.experimental import pallas as pl
from jax.experimental.pallas import tpu as pltpu
from jax.sharding import PartitionSpec as P


epsilon = 1e-05
LANES = 128
NT = (((1,), (1,)), ((), ()))
TN = (((0,), (0,)), ((), ()))


def mm(a, b, dims=(((1,), (0,)), ((), ())), precision=None):
    return lax.dot_general(
        a, b, dims, precision=precision, preferred_element_type=jnp.float32
    )


def scan_kernel(
    starts, place, prep_ref, x_ref, g_ref, b_ref, c_ref, init_ref, same_ref, core_ref, row_ref, far_ref,
    state, src, first_src, *, heads, requests
):
    span, width = x_ref.shape
    tok = same_ref.shape[1]
    head_dim = width // heads
    c0 = pl.program_id(0) * span
    steps = prep_ref[0:8, :]
    run = prep_ref[8:16, :]
    lane = lax.broadcasted_iota(jnp.int32, run.shape, 1)
    shift = 1
    while shift < span:
        run = run + jnp.where(lane >= shift, pltpu.roll(run, shift, 1), 0.0)
        shift *= 2
    before = jnp.zeros_like(run)
    first_last = jnp.int32(0)
    pos = lax.broadcasted_iota(jnp.int32, (span, 1), 0) + c0
    first = jnp.zeros_like(pos)
    inside = []
    for r in range(requests):
        start = starts[r]
        at = start - c0
        here = jnp.logical_and(at >= 0, at < span)
        inside.append(here)
        value = jnp.sum(jnp.where(lane == at - 1, run, 0.0), axis=1, keepdims=True)
        from_here = jnp.where(here, at, span)
        before = jnp.where(lane >= from_here, value, before)
        first_last = jnp.where(at < span, start, first_last)
        first = jnp.where(pos >= start, start, first)
    weight = jnp.exp(run - before)
    last = jnp.where(lane >= first_last - c0, jnp.exp(run[:, span - 1 : span] - run), 0.0)

    spread_row = lax.broadcasted_iota(jnp.int32, (8, width), 0)
    spread_col = lax.broadcasted_iota(jnp.int32, (8, width), 1) // head_dim
    spread = jnp.where(spread_row == spread_col, 1.0, 0.0)

    def widen(rows):
        return mm(rows, spread, TN, lax.Precision.HIGHEST)

    @pl.when(pl.program_id(0) == 0)
    def _():
        state[...] = jnp.zeros_like(state)

    drive = x_ref[...].astype(jnp.float32) * widen(steps)
    drive_low = drive.astype(jnp.bfloat16)
    drive_last = (drive * widen(last)).astype(jnp.bfloat16)
    basis = b_ref[...]
    readout = c_ref[...]
    row = lax.broadcasted_iota(jnp.int32, (span, span), 0)
    col = lax.broadcasted_iota(jnp.int32, (span, span), 1)
    valid = jnp.logical_and(col <= row, col >= first - c0)
    scores = jnp.where(valid, mm(readout, basis, NT), 0.0)

    src[...] = mm(readout, state[...].astype(jnp.bfloat16))
    first_src[...] = state[...]
    for r in range(requests):

        @pl.when(inside[r])
        def _(r=r):
            init = init_ref[r].T
            mine = mm(readout, init.astype(jnp.bfloat16))
            src[...] = jnp.where(first == starts[r], mine, src[...])
            first_src[...] = init

    weight_wide = widen(weight)
    run_cols = run.T
    per_tile = LANES // head_dim
    tile_lane = lax.broadcasted_iota(jnp.int32, (span, LANES), 1) // head_dim
    pieces = []
    for tile in range(heads // per_tile):
        drive_tile = drive_low[:, tile * LANES : (tile + 1) * LANES]
        piece = None
        for j in range(per_tile):
            h = tile * per_tile + j
            gap = jnp.minimum(run_cols[:, h : h + 1] - run[h : h + 1, :], 0.0)
            part = mm((jnp.exp(gap) * scores).astype(jnp.bfloat16), drive_tile)
            piece = part if piece is None else jnp.where(tile_lane == j, part, piece)
        pieces.append(piece)
    inner = pieces[0] if len(pieces) == 1 else jnp.concatenate(pieces, axis=1)
    output = inner + weight_wide * src[...]
    state[...] = mm(basis, drive_last, TN) + weight_wide[span - 1 : span, :] * first_src[...]
    gate = g_ref[...].astype(jnp.float32)
    gated = (output * (gate / (1.0 + jnp.exp(-gate)))).astype(jnp.bfloat16)
    even = place[2] == 0
    mine = jnp.where(even, gated[:tok], gated[tok:])
    other = jnp.where(even, gated[tok:], gated[:tok])
    my_row = lax.rem(pl.program_id(0), 2) == place[1]

    @pl.when(my_row)
    def _():
        same_ref[0] = mine
        core_ref[0] = other

    @pl.when(jnp.logical_not(my_row))
    def _():
        row_ref[0] = mine
        far_ref[0] = other


def scan_heads(head_in, gate_in, in_basis, out_basis, step, rate, init, lengths, place, depth):
    tokens, width = head_in.shape
    heads = step.shape[0]
    requests = lengths.shape[0]
    states = in_basis.shape[1]
    tok = tokens // (4 * depth)
    span = 2 * tok
    ends = jnp.cumsum(lengths)
    starts = (ends - lengths).astype(jnp.int32)
    pad = ((0, 8 - heads), (0, 0))
    prep = jnp.concatenate([jnp.pad(step, pad), jnp.pad(-step * rate[:, None], pad)], axis=0)
    init = init.reshape(requests, width, states)
    cost = pl.CostEstimate(
        flops=2 * tokens * width * (span * 2 + 3 * states),
        bytes_accessed=6 * tokens * width,
        transcendentals=tokens * span * heads,
    )

    def row_block(i, starts, place):
        return (i, 0)

    def out_block(i, starts, place):
        return (lax.rem(place[0] - lax.div(i, 2) + depth, depth), 0, 0)

    return pl.pallas_call(
        functools.partial(scan_kernel, heads=heads, requests=requests),
        out_shape=[jax.ShapeDtypeStruct((depth, tok, width), jnp.bfloat16)] * 4,
        grid_spec=pltpu.PrefetchScalarGridSpec(
            num_scalar_prefetch=2,
            grid=(tokens // span,),
            in_specs=[
                pl.BlockSpec((16, span), lambda i, starts, place: (0, i)),
                pl.BlockSpec((span, width), row_block),
                pl.BlockSpec((span, width), row_block),
                pl.BlockSpec((span, states), row_block),
                pl.BlockSpec((span, states), row_block),
                pl.BlockSpec((requests, width, states), lambda i, starts, place: (0, 0, 0)),
            ],
            out_specs=[pl.BlockSpec((1, tok, width), out_block)] * 4,
            scratch_shapes=[
                pltpu.VMEM((states, width), jnp.float32),
                pltpu.VMEM((span, width), jnp.float32),
                pltpu.VMEM((states, width), jnp.float32),
            ],
        ),
        cost_estimate=cost,
        name="scan",
    )(starts, place, prep, head_in, gate_in, in_basis, out_basis, init)


def project_kernel(*refs, depth, squared):
    acts, weights = refs[:4], refs[4:8]
    outs, squares = refs[8 : 8 + depth], refs[8 + depth :]
    _, tok, width = acts[0].shape
    total = None
    for act, weight in zip(acts, weights):
        part = mm(act[...].reshape(depth * tok, width), weight[...])
        total = part if total is None else total + part
    for dz in range(depth):
        outs[dz][...] = total[dz * tok : (dz + 1) * tok].astype(jnp.bfloat16)
    if squared:

        @pl.when(pl.program_id(0) == 0)
        def _():
            for dz in range(depth):
                wide = [act[dz].astype(jnp.float32) for act in acts]
                summed = sum(jnp.sum(w * w, axis=1, keepdims=True) for w in wide)
                squares[dz][...] = jnp.broadcast_to(summed, (tok, LANES))


def project(acts, weights, half, halves, squared):
    depth, tok, width = acts[0].shape
    model = weights[0].shape[1]
    steps = 2
    columns = model // halves // steps
    cost = pl.CostEstimate(
        flops=8 * depth * tok * width * model // halves,
        bytes_accessed=2 * (4 * width * model + depth * tok * (model + 4 * width)) // halves,
        transcendentals=0,
    )
    out_shape = [jax.ShapeDtypeStruct((tok, columns * steps), jnp.bfloat16)] * depth
    out_specs = [pl.BlockSpec((tok, columns), lambda i: (0, i))] * depth
    if squared:
        out_shape += [jax.ShapeDtypeStruct((tok, LANES), jnp.float32)] * depth
        out_specs += [pl.BlockSpec((tok, LANES), lambda i: (0, 0))] * depth
    out = pl.pallas_call(
        functools.partial(project_kernel, depth=depth, squared=squared),
        out_shape=out_shape,
        grid=(steps,),
        in_specs=[pl.BlockSpec((depth, tok, width), lambda i: (0, 0, 0))] * 4
        + [pl.BlockSpec((width, columns), lambda i: (0, half * steps + i))] * 4,
        out_specs=out_specs,
        cost_estimate=cost,
        name="project",
    )(*acts, *weights)
    return out[:depth], out[depth:]


def expert_kernel(place, *refs, blocks, cap, slots):
    x_refs = refs[:blocks]
    gate_ref, up_ref, down_ref = refs[blocks : blocks + 3]
    outs = refs[blocks + 3 : 2 * blocks + 3]
    rows, total, combine, results = refs[2 * blocks + 3 :]
    expert, part = pl.program_id(0), pl.program_id(1)
    tok, model = outs[0].shape
    count = rows.shape[0]
    wide = count * cap

    @pl.when(jnp.logical_and(expert == 0, part == 0))
    def _():
        here = place[3] * count + lax.broadcasted_iota(jnp.int32, (LANES, wide), 1) // cap
        source = lax.broadcasted_iota(jnp.int32, (LANES, wide), 0)
        pick = jnp.where(jnp.logical_or(source == here, source == here + slots), 1.0, 0.0)
        pick = pick.astype(jnp.bfloat16)
        below = lax.broadcasted_iota(jnp.int32, (tok, tok), 0)
        across = lax.broadcasted_iota(jnp.int32, (tok, tok), 1)
        earlier = jnp.where(across < below, 1.0, 0.0).astype(jnp.bfloat16)
        slot = (lax.broadcasted_iota(jnp.int32, (tok, wide), 1) % cap).astype(jnp.float32)
        for b in range(blocks):
            weight = mm(x_refs[b][:, model : model + LANES], pick)
            chosen = weight > 0.0
            rank = mm(earlier, jnp.where(chosen, 1.0, 0.0).astype(jnp.bfloat16))
            match = jnp.logical_and(chosen, rank == slot)
            select = jnp.where(match, 1.0, 0.0).astype(jnp.bfloat16)
            picked = mm(select, x_refs[b][:, :model], TN).astype(jnp.bfloat16)
            for e in range(count):
                rows[e, b * cap : (b + 1) * cap, :] = picked[e * cap : (e + 1) * cap]
            weight = jnp.where(match, weight, 0.0)
            high = weight.astype(jnp.bfloat16)
            low = (weight - high.astype(jnp.float32)).astype(jnp.bfloat16)
            combine[b] = jnp.concatenate([high, low], axis=1)

    x = rows[expert]
    gate = mm(x, gate_ref[0])
    up = mm(x, up_ref[0])
    act = (gate / (1.0 + jnp.exp(-gate)) * up).astype(jnp.bfloat16)
    down = mm(act, down_ref[0])

    @pl.when(part == 0)
    def _():
        total[...] = down

    @pl.when(part > 0)
    def _():
        total[...] += down

    @pl.when(part == pl.num_programs(1) - 1)
    def _():
        for b in range(blocks):
            value = total[b * cap : (b + 1) * cap, :].astype(jnp.bfloat16)
            results[b, pl.ds(pl.multiple_of(expert * cap, cap), cap), :] = value
            results[b, pl.ds(pl.multiple_of(wide + expert * cap, cap), cap), :] = value

    @pl.when(jnp.logical_and(expert == count - 1, part == pl.num_programs(1) - 1))
    def _():
        for b in range(blocks):
            outs[b][...] = mm(combine[b], results[b]).astype(jnp.bfloat16)


def run_experts(xs, w_gate, w_up, w_down, place, cap, slots, parts):
    blocks = len(xs)
    tok, extended = xs[0].shape
    count, model, hidden = w_gate.shape
    tile = hidden // parts
    cost = pl.CostEstimate(
        flops=6 * count * blocks * cap * model * hidden,
        bytes_accessed=6 * count * model * hidden + 4 * blocks * tok * model,
        transcendentals=count * blocks * cap * hidden,
    )
    return pl.pallas_call(
        functools.partial(expert_kernel, blocks=blocks, cap=cap, slots=slots),
        out_shape=[jax.ShapeDtypeStruct((tok, model), jnp.bfloat16)] * blocks,
        grid_spec=pltpu.PrefetchScalarGridSpec(
            num_scalar_prefetch=1,
            grid=(count, parts),
            in_specs=[pl.BlockSpec((tok, extended), lambda e, f, place: (0, 0))] * blocks
            + [
                pl.BlockSpec((1, model, tile), lambda e, f, place: (e, 0, f)),
                pl.BlockSpec((1, model, tile), lambda e, f, place: (e, 0, f)),
                pl.BlockSpec((1, tile, model), lambda e, f, place: (e, f, 0)),
            ],
            out_specs=[pl.BlockSpec((tok, model), lambda e, f, place: (0, 0))] * blocks,
            scratch_shapes=[
                pltpu.VMEM((count, blocks * cap, model), jnp.bfloat16),
                pltpu.VMEM((blocks * cap, model), jnp.float32),
                pltpu.VMEM((blocks, tok, 2 * count * cap), jnp.bfloat16),
                pltpu.VMEM((blocks, 2 * count * cap, model), jnp.bfloat16),
            ],
        ),
        compiler_params=pltpu.CompilerParams(vmem_limit_bytes=40 * 1024 * 1024),
        cost_estimate=cost,
        name="experts",
    )(place, *xs, w_gate, w_up, w_down)


def add_low(a, b):
    return (a.astype(jnp.float32) + b.astype(jnp.float32)).astype(jnp.bfloat16)


def local(
    resid_in, head_in, gate_in, in_basis, out_basis, step_size, decay_rate, init_state, lengths,
    norm_gain, out_proj, moe_gain, expert_ids, route_weight, placement, w_gate, w_up, w_down,
):
    devices = lax.axis_size("mix")
    depth = devices // 4
    me = lax.axis_index("mix")
    place = jnp.stack([me // 4, (me // 2) % 2, me % 2, me]).astype(jnp.int32)
    tokens = head_in.shape[0]
    tok = tokens // devices
    width = head_in.shape[1]

    def cross(x, mask):
        return lax.ppermute(x, "mix", [(i, i ^ mask) for i in range(devices)])

    def onward(x):
        return lax.ppermute(x, "mix", [(i, (i + 4) % devices) for i in range(devices)])

    gain = lax.dynamic_slice(norm_gain, (me * width,), (width,))
    proj = (out_proj.astype(jnp.float32) * gain[:, None]).astype(jnp.bfloat16)
    proj_y = cross(proj, 2)

    slots = placement.shape[0]
    slot_of = jnp.sum(
        jnp.where(
            expert_ids[:, :, None] == jnp.arange(slots, dtype=jnp.int32), placement[None, None, :], 0
        ),
        axis=2,
    )
    route = jnp.sum(
        jnp.where(
            slot_of[:, :, None] == jnp.arange(slots, dtype=jnp.int32), route_weight[:, :, None], 0.0
        ),
        axis=1,
    )
    route_high = lax.reduce_precision(route, 8, 7)
    table = jnp.concatenate([route_high, route - route_high], axis=1)
    table = jnp.pad(table, ((0, 0), (0, LANES - 2 * slots))).astype(jnp.bfloat16)

    gated = scan_heads(
        head_in, gate_in, in_basis, out_basis, step_size, decay_rate, init_state, lengths,
        place, depth,
    )
    projs = [proj, cross(proj, 1), proj_y, cross(proj_y, 1)]
    acts = [gated[0], cross(gated[1], 1), cross(gated[2], 2), cross(gated[3], 3)]
    halves = 2
    sums = []
    for half in range(halves):
        mixed, squares = project(acts, projs, half, halves, half == 0)
        total = mixed[1]
        if half == 0:
            norm = squares[1]
        for dz in range(2, depth):
            total = add_low(onward(total), mixed[dz])
            if half == 0:
                norm = onward(norm) + squares[dz]
        total = onward(total).astype(jnp.float32) + mixed[0].astype(jnp.float32)
        if half == 0:
            norm = (onward(norm) + squares[0])[:, 0:1]
        sums.append(total)
    mixer_sum = jnp.concatenate(sums, axis=1)
    hidden = resid_in.astype(jnp.float32) + mixer_sum * lax.rsqrt(norm / (devices * width) + epsilon)
    normed = (
        hidden * lax.rsqrt(jnp.mean(hidden * hidden, axis=1, keepdims=True) + epsilon) * moe_gain
    ).astype(jnp.bfloat16)
    mine = jnp.concatenate([normed, table], axis=1)

    cap = 2 * tok * expert_ids.shape[1] // slots
    sums = []
    for dz in range(depth):
        if dz > 0:
            mine = onward(mine)
        other = cross(mine, 2)
        block = [mine, cross(mine, 1), other, cross(other, 1)]
        outs = run_experts(block, w_gate, w_up, w_down, place, cap, slots, 1)
        near = add_low(outs[0], cross(outs[1], 1))
        far = add_low(outs[2], cross(outs[3], 1))
        sums.append(add_low(near, cross(far, 2)))
    total = sums[1]
    for dz in range(2, depth):
        total = add_low(onward(total), sums[dz])
    expert_sum = onward(total).astype(jnp.float32) + sums[0].astype(jnp.float32)
    return (hidden + expert_sum).astype(jnp.bfloat16)


def solution(mesh):
    return jax.shard_map(
        local,
        mesh=mesh,
        in_specs=(
            P(("groups", "mix"), None),
            P("groups", "mix"),
            P("groups", "mix"),
            P("groups", None),
            P("groups", None),
            P("mix", "groups"),
            P("mix"),
            P("groups", "mix", None, None),
            P("groups"),
            P(),
            P("mix", None),
            P(),
            P(("groups", "mix"), None),
            P(("groups", "mix"), None),
            P(),
            P("mix", None, None),
            P("mix", None, None),
            P("mix", None, None),
        ),
        out_specs=P(("groups", "mix"), None),
        check_vma=False,
    )
```

```python
import functools

import jax
import jax.numpy as jnp
from jax import lax
from jax.experimental import pallas as pl
from jax.experimental.pallas import tpu as pltpu
from jax.sharding import PartitionSpec as P


epsilon = 1e-05
LANES = 128
NT = (((1,), (1,)), ((), ()))
TN = (((0,), (0,)), ((), ()))


def mm(a, b, dims=(((1,), (0,)), ((), ())), precision=None):
    return lax.dot_general(
        a, b, dims, precision=precision, preferred_element_type=jnp.float32
    )


def scan_kernel(
    starts, place, prep_ref, x_ref, g_ref, b_ref, c_ref, init_ref, *refs, heads, requests
):
    out_refs, (state, src, first_src) = refs[:8], refs[8:]
    span, width = x_ref.shape
    tok = out_refs[0].shape[1]
    head_dim = width // heads
    c0 = pl.program_id(0) * span
    steps = prep_ref[0:8, :]
    run = prep_ref[8:16, :]
    lane = lax.broadcasted_iota(jnp.int32, run.shape, 1)
    shift = 1
    while shift < span:
        run = run + jnp.where(lane >= shift, pltpu.roll(run, shift, 1), 0.0)
        shift *= 2
    before = jnp.zeros_like(run)
    first_last = jnp.int32(0)
    pos = lax.broadcasted_iota(jnp.int32, (span, 1), 0) + c0
    first = jnp.zeros_like(pos)
    inside = []
    for r in range(requests):
        start = starts[r]
        at = start - c0
        here = jnp.logical_and(at >= 0, at < span)
        inside.append(here)
        value = jnp.sum(jnp.where(lane == at - 1, run, 0.0), axis=1, keepdims=True)
        from_here = jnp.where(here, at, span)
        before = jnp.where(lane >= from_here, value, before)
        first_last = jnp.where(at < span, start, first_last)
        first = jnp.where(pos >= start, start, first)
    weight = jnp.exp(run - before)
    last = jnp.where(lane >= first_last - c0, jnp.exp(run[:, span - 1 : span] - run), 0.0)

    spread_row = lax.broadcasted_iota(jnp.int32, (8, width), 0)
    spread_col = lax.broadcasted_iota(jnp.int32, (8, width), 1) // head_dim
    spread = jnp.where(spread_row == spread_col, 1.0, 0.0)

    def widen(rows):
        return mm(rows, spread, TN, lax.Precision.HIGHEST)

    @pl.when(pl.program_id(0) == 0)
    def _():
        state[...] = jnp.zeros_like(state)

    drive = x_ref[...].astype(jnp.float32) * widen(steps)
    drive_low = drive.astype(jnp.bfloat16)
    drive_last = (drive * widen(last)).astype(jnp.bfloat16)
    basis = b_ref[...]
    readout = c_ref[...]
    row = lax.broadcasted_iota(jnp.int32, (span, span), 0)
    col = lax.broadcasted_iota(jnp.int32, (span, span), 1)
    valid = jnp.logical_and(col <= row, col >= first - c0)
    scores = jnp.where(valid, mm(readout, basis, NT), 0.0)

    src[...] = mm(readout, state[...].astype(jnp.bfloat16))
    first_src[...] = state[...]
    for r in range(requests):

        @pl.when(inside[r])
        def _(r=r):
            init = init_ref[r].T
            mine = mm(readout, init.astype(jnp.bfloat16))
            src[...] = jnp.where(first == starts[r], mine, src[...])
            first_src[...] = init

    weight_wide = widen(weight)
    run_cols = run.T
    per_tile = LANES // head_dim
    tile_lane = lax.broadcasted_iota(jnp.int32, (span, LANES), 1) // head_dim
    pieces = []
    for tile in range(heads // per_tile):
        drive_tile = drive_low[:, tile * LANES : (tile + 1) * LANES]
        piece = None
        for j in range(per_tile):
            h = tile * per_tile + j
            gap = jnp.minimum(run_cols[:, h : h + 1] - run[h : h + 1, :], 0.0)
            part = mm((jnp.exp(gap) * scores).astype(jnp.bfloat16), drive_tile)
            piece = part if piece is None else jnp.where(tile_lane == j, part, piece)
        pieces.append(piece)
    inner = pieces[0] if len(pieces) == 1 else jnp.concatenate(pieces, axis=1)
    output = inner + weight_wide * src[...]
    state[...] = mm(basis, drive_last, TN) + weight_wide[span - 1 : span, :] * first_src[...]
    gate = g_ref[...].astype(jnp.float32)
    gated = (output * (gate / (1.0 + jnp.exp(-gate)))).astype(jnp.bfloat16)
    even = lax.rem(place[0], 2) == 0
    mine = jnp.where(even, gated[:tok], gated[tok:])
    other = jnp.where(even, gated[tok:], gated[:tok])
    pair = lax.rem(pl.program_id(0), 4) ^ lax.div(lax.rem(place[0], 8), 2)
    for way in range(4):

        @pl.when(pair == way)
        def _(way=way):
            out_refs[2 * way][0] = mine
            out_refs[2 * way + 1][0] = other


def scan_heads(head_in, gate_in, in_basis, out_basis, step, rate, init, lengths, place, depth):
    tokens, width = head_in.shape
    heads = step.shape[0]
    requests = lengths.shape[0]
    states = in_basis.shape[1]
    tok = tokens // (8 * depth)
    span = 2 * tok
    ends = jnp.cumsum(lengths)
    starts = (ends - lengths).astype(jnp.int32)
    pad = ((0, 8 - heads), (0, 0))
    prep = jnp.concatenate([jnp.pad(step, pad), jnp.pad(-step * rate[:, None], pad)], axis=0)
    init = init.reshape(requests, width, states)
    cost = pl.CostEstimate(
        flops=2 * tokens * width * (span * 2 + 3 * states),
        bytes_accessed=6 * tokens * width,
        transcendentals=tokens * span * heads,
    )

    def row_block(i, starts, place):
        return (i, 0)

    def out_block(i, starts, place):
        return (lax.rem(lax.div(place[0], 8) - lax.div(i, 4) + depth, depth), 0, 0)

    return pl.pallas_call(
        functools.partial(scan_kernel, heads=heads, requests=requests),
        out_shape=[jax.ShapeDtypeStruct((depth, tok, width), jnp.bfloat16)] * 8,
        grid_spec=pltpu.PrefetchScalarGridSpec(
            num_scalar_prefetch=2,
            grid=(tokens // span,),
            in_specs=[
                pl.BlockSpec((16, span), lambda i, starts, place: (0, i)),
                pl.BlockSpec((span, width), row_block),
                pl.BlockSpec((span, width), row_block),
                pl.BlockSpec((span, states), row_block),
                pl.BlockSpec((span, states), row_block),
                pl.BlockSpec((requests, width, states), lambda i, starts, place: (0, 0, 0)),
            ],
            out_specs=[pl.BlockSpec((1, tok, width), out_block)] * 8,
            scratch_shapes=[
                pltpu.VMEM((states, width), jnp.float32),
                pltpu.VMEM((span, width), jnp.float32),
                pltpu.VMEM((states, width), jnp.float32),
            ],
        ),
        cost_estimate=cost,
        name="scan",
    )(starts, place, prep, head_in, gate_in, in_basis, out_basis, init)


def project_kernel(*refs, depth, squared):
    gain_ref, acts, refs = refs[0], refs[1:9], refs[9:]
    weights, refs = refs[:10], refs[10:]
    outs, squares = refs[:depth], refs[depth:]
    _, tok, width = acts[0].shape
    total = None
    for mask, act in enumerate(acts):
        rows = act[...].reshape(depth * tok, width).astype(jnp.float32)
        rows = (rows * gain_ref[mask : mask + 1, :]).astype(jnp.bfloat16)
        if mask < 6:
            part = mm(rows, weights[mask][...])
        else:
            halves = weights[6 + mask % 2], weights[8 + mask % 2]
            part = mm(rows, jnp.concatenate([h[...] for h in halves], axis=0))
        total = part if total is None else total + part
    for dz in range(depth):
        outs[dz][...] = total[dz * tok : (dz + 1) * tok].astype(jnp.bfloat16)
    if squared:

        @pl.when(pl.program_id(0) == 0)
        def _():
            for dz in range(depth):
                wide = [act[dz].astype(jnp.float32) for act in acts]
                summed = sum(jnp.sum(w * w, axis=1, keepdims=True) for w in wide)
                squares[dz][...] = jnp.broadcast_to(summed, (tok, LANES))


def project(gains, acts, weights, half, halves, squared):
    depth, tok, width = acts[0].shape
    model = weights[0].shape[1]
    steps = 2
    columns = model // halves // steps
    cost = pl.CostEstimate(
        flops=16 * depth * tok * width * model // halves,
        bytes_accessed=2 * (8 * width * model + depth * tok * (model + 8 * width)) // halves,
        transcendentals=0,
    )
    out_shape = [jax.ShapeDtypeStruct((tok, columns * steps), jnp.bfloat16)] * depth
    out_specs = [pl.BlockSpec((tok, columns), lambda i: (0, i))] * depth
    if squared:
        out_shape += [jax.ShapeDtypeStruct((tok, LANES), jnp.float32)] * depth
        out_specs += [pl.BlockSpec((tok, LANES), lambda i: (0, 0))] * depth
    out = pl.pallas_call(
        functools.partial(project_kernel, depth=depth, squared=squared),
        out_shape=out_shape,
        grid=(steps,),
        in_specs=[pl.BlockSpec((8, width), lambda i: (0, 0))]
        + [pl.BlockSpec((depth, tok, width), lambda i: (0, 0, 0))] * 8
        + [pl.BlockSpec((w.shape[0], columns), lambda i: (0, half * steps + i)) for w in weights],
        out_specs=out_specs,
        cost_estimate=cost,
        name="project",
    )(gains, *acts, *weights)
    return out[:depth], out[depth:]


def expert_kernel(place, *refs, blocks, cap, slots):
    x_refs = refs[:blocks]
    gate_ref, up_ref, down_ref = refs[blocks : blocks + 3]
    outs = refs[blocks + 3 : 2 * blocks + 3]
    rows, total, combine, results = refs[2 * blocks + 3 :]
    expert, part = pl.program_id(0), pl.program_id(1)
    tok, model = outs[0].shape
    count = rows.shape[0]
    wide = count * cap

    @pl.when(jnp.logical_and(expert == 0, part == 0))
    def _():
        here = place[0] * count + lax.broadcasted_iota(jnp.int32, (LANES, wide), 1) // cap
        source = lax.broadcasted_iota(jnp.int32, (LANES, wide), 0)
        pick = jnp.where(jnp.logical_or(source == here, source == here + slots), 1.0, 0.0)
        pick = pick.astype(jnp.bfloat16)
        below = lax.broadcasted_iota(jnp.int32, (tok, tok), 0)
        across = lax.broadcasted_iota(jnp.int32, (tok, tok), 1)
        earlier = jnp.where(across < below, 1.0, 0.0).astype(jnp.bfloat16)
        slot = (lax.broadcasted_iota(jnp.int32, (tok, wide), 1) % cap).astype(jnp.float32)
        for b in range(blocks):
            weight = mm(x_refs[b][:, model : model + LANES], pick)
            chosen = weight > 0.0
            rank = mm(earlier, jnp.where(chosen, 1.0, 0.0).astype(jnp.bfloat16))
            match = jnp.logical_and(chosen, rank == slot)
            select = jnp.where(match, 1.0, 0.0).astype(jnp.bfloat16)
            picked = mm(select, x_refs[b][:, :model], TN).astype(jnp.bfloat16)
            for e in range(count):
                rows[e, b * cap : (b + 1) * cap, :] = picked[e * cap : (e + 1) * cap]
            weight = jnp.where(match, weight, 0.0)
            high = weight.astype(jnp.bfloat16)
            low = (weight - high.astype(jnp.float32)).astype(jnp.bfloat16)
            combine[b] = jnp.concatenate([high, low], axis=1)

    x = rows[expert]
    gate = mm(x, gate_ref[0])
    up = mm(x, up_ref[0])
    act = (gate / (1.0 + jnp.exp(-gate)) * up).astype(jnp.bfloat16)
    down = mm(act, down_ref[0])

    @pl.when(part == 0)
    def _():
        total[...] = down

    @pl.when(part > 0)
    def _():
        total[...] += down

    @pl.when(part == pl.num_programs(1) - 1)
    def _():
        for b in range(blocks):
            value = total[b * cap : (b + 1) * cap, :].astype(jnp.bfloat16)
            results[b, pl.ds(pl.multiple_of(expert * cap, cap), cap), :] = value
            results[b, pl.ds(pl.multiple_of(wide + expert * cap, cap), cap), :] = value

    @pl.when(jnp.logical_and(expert == count - 1, part == pl.num_programs(1) - 1))
    def _():
        for b in range(blocks):
            outs[b][...] = mm(combine[b], results[b]).astype(jnp.bfloat16)


def run_experts(xs, w_gate, w_up, w_down, place, cap, slots, parts):
    blocks = len(xs)
    tok, extended = xs[0].shape
    count, model, hidden = w_gate.shape
    tile = hidden // parts
    cost = pl.CostEstimate(
        flops=6 * count * blocks * cap * model * hidden,
        bytes_accessed=6 * count * model * hidden + 4 * blocks * tok * model,
        transcendentals=count * blocks * cap * hidden,
    )
    return pl.pallas_call(
        functools.partial(expert_kernel, blocks=blocks, cap=cap, slots=slots),
        out_shape=[jax.ShapeDtypeStruct((tok, model), jnp.bfloat16)] * blocks,
        grid_spec=pltpu.PrefetchScalarGridSpec(
            num_scalar_prefetch=1,
            grid=(count, parts),
            in_specs=[pl.BlockSpec((tok, extended), lambda e, f, place: (0, 0))] * blocks
            + [
                pl.BlockSpec((1, model, tile), lambda e, f, place: (e, 0, f)),
                pl.BlockSpec((1, model, tile), lambda e, f, place: (e, 0, f)),
                pl.BlockSpec((1, tile, model), lambda e, f, place: (e, f, 0)),
            ],
            out_specs=[pl.BlockSpec((tok, model), lambda e, f, place: (0, 0))] * blocks,
            scratch_shapes=[
                pltpu.VMEM((count, blocks * cap, model), jnp.bfloat16),
                pltpu.VMEM((blocks * cap, model), jnp.float32),
                pltpu.VMEM((blocks, tok, 2 * count * cap), jnp.bfloat16),
                pltpu.VMEM((blocks, 2 * count * cap, model), jnp.bfloat16),
            ],
        ),
        compiler_params=pltpu.CompilerParams(vmem_limit_bytes=40 * 1024 * 1024),
        cost_estimate=cost,
        name="experts",
    )(place, *xs, w_gate, w_up, w_down)


def add_low(a, b):
    return (a.astype(jnp.float32) + b.astype(jnp.float32)).astype(jnp.bfloat16)


def local(
    resid_in, head_in, gate_in, in_basis, out_basis, step_size, decay_rate, init_state, lengths,
    norm_gain, out_proj, moe_gain, expert_ids, route_weight, placement, w_gate, w_up, w_down,
):
    devices = lax.axis_size("mix")
    depth = devices // 4
    me = lax.axis_index("mix")
    place = me.astype(jnp.int32)[None]
    tokens = head_in.shape[0]
    tok = tokens // devices
    width = head_in.shape[1]

    def cross(x, mask):
        return lax.ppermute(x, "mix", [(i, i ^ mask) for i in range(devices)])

    def onward(x, stride=4):
        return lax.ppermute(x, "mix", [(i, (i + stride) % devices) for i in range(devices)])

    proj_y, proj_z = cross(out_proj, 2), cross(out_proj, 4)
    proj_yz = (cross(proj_y[: width // 2], 4), cross(proj_z[width // 2 :], 2))
    gains = jnp.take(norm_gain.reshape(devices, width), me ^ jnp.arange(8), axis=0)

    slots = placement.shape[0]
    slot_of = jnp.sum(
        jnp.where(
            expert_ids[:, :, None] == jnp.arange(slots, dtype=jnp.int32), placement[None, None, :], 0
        ),
        axis=2,
    )
    route = jnp.sum(
        jnp.where(
            slot_of[:, :, None] == jnp.arange(slots, dtype=jnp.int32), route_weight[:, :, None], 0.0
        ),
        axis=1,
    )
    route_high = lax.reduce_precision(route, 8, 7)
    table = jnp.concatenate([route_high, route - route_high], axis=1)
    table = jnp.pad(table, ((0, 0), (0, LANES - 2 * slots))).astype(jnp.bfloat16)

    gated = scan_heads(
        head_in, gate_in, in_basis, out_basis, step_size, decay_rate, init_state, lengths,
        place, depth // 2,
    )
    projs = []
    for block in (out_proj, proj_y, proj_z, *proj_yz):
        projs += [block, cross(block, 1)]
    acts = [gated[0]] + [cross(gated[mask], mask) for mask in range(1, 8)]
    halves = 2
    sums = []
    for half in range(halves):
        mixed, squares = project(gains, acts, projs, half, halves, half == 0)
        total = mixed[1]
        if half == 0:
            norm = squares[1]
        for dz in range(2, depth // 2):
            total = add_low(onward(total, 8), mixed[dz])
            if half == 0:
                norm = onward(norm, 8) + squares[dz]
        total = onward(total, 8).astype(jnp.float32) + mixed[0].astype(jnp.float32)
        if half == 0:
            norm = (onward(norm, 8) + squares[0])[:, 0:1]
        sums.append(total)
    mixer_sum = jnp.concatenate(sums, axis=1)
    hidden = resid_in.astype(jnp.float32) + mixer_sum * lax.rsqrt(norm / (devices * width) + epsilon)
    normed = (
        hidden * lax.rsqrt(jnp.mean(hidden * hidden, axis=1, keepdims=True) + epsilon) * moe_gain
    ).astype(jnp.bfloat16)
    mine = jnp.concatenate([normed, table], axis=1)

    cap = 2 * tok * expert_ids.shape[1] // slots
    sums = []
    for dz in range(depth):
        if dz > 0:
            mine = onward(mine)
        other = cross(mine, 2) if dz < depth - 1 else onward(other)
        block = [mine, cross(mine, 1), other, cross(other, 1)]
        outs = run_experts(block, w_gate, w_up, w_down, place, cap, slots, 1)
        near = add_low(outs[0], cross(outs[1], 1))
        far = add_low(outs[2], cross(outs[3], 1))
        sums.append(add_low(near, cross(far, 2)))
    total = sums[1]
    for dz in range(2, depth):
        total = add_low(onward(total), sums[dz])
    expert_sum = onward(total).astype(jnp.float32) + sums[0].astype(jnp.float32)
    return (hidden + expert_sum).astype(jnp.bfloat16)


def solution(mesh):
    return jax.shard_map(
        local,
        mesh=mesh,
        in_specs=(
            P(("groups", "mix"), None),
            P("groups", "mix"),
            P("groups", "mix"),
            P("groups", None),
            P("groups", None),
            P("mix", "groups"),
            P("mix"),
            P("groups", "mix", None, None),
            P("groups"),
            P(),
            P("mix", None),
            P(),
            P(("groups", "mix"), None),
            P(("groups", "mix"), None),
            P(),
            P("mix", None, None),
            P("mix", None, None),
            P("mix", None, None),
        ),
        out_specs=P(("groups", "mix"), None),
        check_vma=False,
    )
```

```python
import functools

import jax
import jax.numpy as jnp
from jax import lax
from jax.experimental import pallas as pl
from jax.experimental.pallas import tpu as pltpu
from jax.sharding import PartitionSpec as P


epsilon = 1e-05
LANES = 128
NT = (((1,), (1,)), ((), ()))
TN = (((0,), (0,)), ((), ()))


def mm(a, b, dims=(((1,), (0,)), ((), ())), precision=None):
    return lax.dot_general(
        a, b, dims, precision=precision, preferred_element_type=jnp.float32
    )


def scan_kernel(
    lengths, place, rates, step_ref, x_ref, g_ref, b_ref, c_ref, init_ref, *refs, span, chunks
):
    out_refs, (runs, rows, state, src, first_src) = refs[:8], refs[8:]
    heads, tokens = step_ref.shape
    requests, width, _ = init_ref.shape
    tok = out_refs[0].shape[1]
    head_dim = width // heads
    starts = [jnp.int32(0)]
    for r in range(requests - 1):
        starts.append(starts[-1] + lengths[r])

    @pl.when(pl.program_id(0) == 0)
    def _():
        state[...] = jnp.zeros_like(state)
        runs[...] = jnp.zeros_like(runs)
        for h in range(heads):
            runs[h : h + 1, :] = -step_ref[h : h + 1, :] * rates[h]
        run = runs[...]
        lane = lax.broadcasted_iota(jnp.int32, run.shape, 1)
        inner = lane % span
        shift = 1
        while shift < span:
            run = run + jnp.where(inner >= shift, pltpu.roll(run, shift, 1), 0.0)
            shift *= 2
        runs[...] = run
        final = lane - inner + (span - 1)
        before = jnp.zeros_like(run)
        first_last = jnp.zeros_like(lane)
        for start in starts:
            end = start - start % span + span
            inside = jnp.logical_and(lane == start - 1, start % span > 0)
            value = jnp.sum(jnp.where(inside, run, 0.0), axis=1, keepdims=True)
            before = jnp.where(jnp.logical_and(lane >= start, lane < end), value, before)
            first_last = jnp.where(final >= start, start, first_last)
        weight = jnp.exp(run - before)
        ends = [
            jnp.broadcast_to(run[:, at + span - 1 : at + span], (8, span))
            for at in range(0, tokens, span)
        ]
        ends = jnp.concatenate(ends, axis=1)
        last = jnp.where(lane >= first_last, jnp.exp(ends - run), 0.0)
        zeros = jnp.zeros_like(run)
        steps = jnp.concatenate([step_ref[...], zeros[heads:]], axis=0)
        for i, value in enumerate((steps, last, weight)):
            high = value.astype(jnp.bfloat16)
            low = (value - high.astype(jnp.float32)).astype(jnp.bfloat16)
            rows[16 * i : 16 * i + 16, :] = jnp.concatenate([high, low], axis=0)

    spread_row = lax.broadcasted_iota(jnp.int32, (48, 3 * width), 0)
    spread_col = lax.broadcasted_iota(jnp.int32, (48, 3 * width), 1)
    spread = jnp.logical_and(
        spread_row // 16 == spread_col // width, spread_row % 8 == spread_col % width // head_dim
    )
    spread = jnp.where(spread, 1.0, 0.0).astype(jnp.bfloat16)
    row = lax.broadcasted_iota(jnp.int32, (span, span), 0)
    col = lax.broadcasted_iota(jnp.int32, (span, span), 1)
    causal = col <= row
    per_tile = LANES // head_dim
    tile_lane = lax.broadcasted_iota(jnp.int32, (span, LANES), 1) // head_dim
    local_pos = lax.broadcasted_iota(jnp.int32, (span, 1), 0)

    for u in range(chunks):
        chunk = pl.program_id(0) * chunks + u
        c0 = pl.multiple_of(chunk * span, span)
        here = pl.ds(u * span, span)
        run = runs[:, pl.ds(c0, span)]
        pos = local_pos + c0
        first = jnp.zeros_like(pos)
        for start in starts:
            first = jnp.where(pos >= start, start, first)
        spread_all = mm(rows[:, pl.ds(c0, span)], spread, TN)
        weight_wide = spread_all[:, 2 * width :]
        drive = x_ref[here, :].astype(jnp.float32) * spread_all[:, :width]
        drive_low = drive.astype(jnp.bfloat16)
        drive_last = (drive * spread_all[:, width : 2 * width]).astype(jnp.bfloat16)
        basis = b_ref[here, :]
        readout = c_ref[here, :]
        valid = jnp.logical_and(causal, col >= first - c0)
        scores = jnp.where(valid, mm(readout, basis, NT), 0.0)

        src[...] = mm(readout, state[...].astype(jnp.bfloat16))
        first_src[...] = state[...]
        for r, start in enumerate(starts):

            @pl.when(jnp.logical_and(start >= c0, start < c0 + span))
            def _(r=r, start=start):
                init = init_ref[r].T
                mine = mm(readout, init.astype(jnp.bfloat16))
                src[...] = jnp.where(first == start, mine, src[...])
                first_src[...] = init

        run_cols = run.T
        pieces = []
        for tile in range(heads // per_tile):
            drive_tile = drive_low[:, tile * LANES : (tile + 1) * LANES]
            piece = None
            for j in range(per_tile):
                h = tile * per_tile + j
                gap = jnp.minimum(run_cols[:, h : h + 1] - run[h : h + 1, :], 0.0)
                part = mm((jnp.exp(gap) * scores).astype(jnp.bfloat16), drive_tile)
                piece = part if piece is None else jnp.where(tile_lane == j, part, piece)
            pieces.append(piece)
        within = pieces[0] if len(pieces) == 1 else jnp.concatenate(pieces, axis=1)
        output = within + weight_wide * src[...]
        state[...] = mm(basis, drive_last, TN) + weight_wide[span - 1 : span, :] * first_src[...]
        gate = g_ref[here, :].astype(jnp.float32)
        gated = (output * (gate / (1.0 + jnp.exp(-gate)))).astype(jnp.bfloat16)
        even = lax.rem(place[0], 2) == 0
        mine = jnp.where(even, gated[:tok], gated[tok:])
        other = jnp.where(even, gated[tok:], gated[:tok])
        pair = lax.rem(chunk, 4) ^ lax.div(lax.rem(place[0], 8), 2)
        for way in range(4):

            @pl.when(pair == way)
            def _(way=way, mine=mine, other=other):
                out_refs[2 * way][0] = mine
                out_refs[2 * way + 1][0] = other


def scan_heads(head_in, gate_in, in_basis, out_basis, step, rate, init, lengths, place, depth):
    tokens, width = head_in.shape
    heads = step.shape[0]
    requests = lengths.shape[0]
    states = in_basis.shape[1]
    tok = tokens // (8 * depth)
    span = 2 * tok
    chunks = 2
    block = chunks * span
    init = init.reshape(requests, width, states)
    cost = pl.CostEstimate(
        flops=2 * tokens * width * (span * 2 + 3 * states),
        bytes_accessed=6 * tokens * width,
        transcendentals=tokens * span * heads,
    )

    def row_block(i, lengths, place, rates):
        return (i, 0)

    def out_block(i, lengths, place, rates):
        return (lax.rem(lax.div(place[0], 8) - lax.div(i * chunks, 4) + depth, depth), 0, 0)

    return pl.pallas_call(
        functools.partial(scan_kernel, span=span, chunks=chunks),
        out_shape=[jax.ShapeDtypeStruct((depth, tok, width), jnp.bfloat16)] * 8,
        grid_spec=pltpu.PrefetchScalarGridSpec(
            num_scalar_prefetch=3,
            grid=(tokens // block,),
            in_specs=[
                pl.BlockSpec((heads, tokens), lambda i, lengths, place, rates: (0, 0)),
                pl.BlockSpec((block, width), row_block),
                pl.BlockSpec((block, width), row_block),
                pl.BlockSpec((block, states), row_block),
                pl.BlockSpec((block, states), row_block),
                pl.BlockSpec((requests, width, states), lambda i, lengths, place, rates: (0, 0, 0)),
            ],
            out_specs=[pl.BlockSpec((1, tok, width), out_block)] * 8,
            scratch_shapes=[
                pltpu.VMEM((8, tokens), jnp.float32),
                pltpu.VMEM((48, tokens), jnp.bfloat16),
                pltpu.VMEM((states, width), jnp.float32),
                pltpu.VMEM((span, width), jnp.float32),
                pltpu.VMEM((states, width), jnp.float32),
            ],
        ),
        cost_estimate=cost,
        name="scan",
    )(lengths, place, rate, step, head_in, gate_in, in_basis, out_basis, init)


def project_kernel(*refs, depth, squared):
    gain_ref, acts, refs = refs[0], refs[1:9], refs[9:]
    weights, refs = refs[:10], refs[10:]
    outs, squares = refs[:depth], refs[depth:]
    _, tok, width = acts[0].shape
    total = None
    for mask, act in enumerate(acts):
        rows = act[...].reshape(depth * tok, width).astype(jnp.float32)
        rows = (rows * gain_ref[mask : mask + 1, :]).astype(jnp.bfloat16)
        if mask < 6:
            part = mm(rows, weights[mask][...])
        else:
            halves = weights[6 + mask % 2], weights[8 + mask % 2]
            part = mm(rows, jnp.concatenate([h[...] for h in halves], axis=0))
        total = part if total is None else total + part
    for dz in range(depth):
        outs[dz][...] = total[dz * tok : (dz + 1) * tok].astype(jnp.bfloat16)
    if squared:

        @pl.when(pl.program_id(0) == 0)
        def _():
            for dz in range(depth):
                wide = [act[dz].astype(jnp.float32) for act in acts]
                summed = sum(jnp.sum(w * w, axis=1, keepdims=True) for w in wide)
                squares[dz][...] = jnp.broadcast_to(summed, (tok, LANES))


def project(gains, acts, weights, half, halves, squared):
    depth, tok, width = acts[0].shape
    model = weights[0].shape[1]
    steps = 2
    columns = model // halves // steps
    cost = pl.CostEstimate(
        flops=16 * depth * tok * width * model // halves,
        bytes_accessed=2 * (8 * width * model + depth * tok * (model + 8 * width)) // halves,
        transcendentals=0,
    )
    out_shape = [jax.ShapeDtypeStruct((tok, columns * steps), jnp.bfloat16)] * depth
    out_specs = [pl.BlockSpec((tok, columns), lambda i: (0, i))] * depth
    if squared:
        out_shape += [jax.ShapeDtypeStruct((tok, LANES), jnp.float32)] * depth
        out_specs += [pl.BlockSpec((tok, LANES), lambda i: (0, 0))] * depth
    out = pl.pallas_call(
        functools.partial(project_kernel, depth=depth, squared=squared),
        out_shape=out_shape,
        grid=(steps,),
        in_specs=[pl.BlockSpec((8, width), lambda i: (0, 0))]
        + [pl.BlockSpec((depth, tok, width), lambda i: (0, 0, 0))] * 8
        + [pl.BlockSpec((w.shape[0], columns), lambda i: (0, half * steps + i)) for w in weights],
        out_specs=out_specs,
        cost_estimate=cost,
        name="project",
    )(gains, *acts, *weights)
    return out[:depth], out[depth:]


def expert_kernel(place, *refs, blocks, cap, slots):
    x_refs = refs[:blocks]
    gate_ref, up_ref, down_ref = refs[blocks : blocks + 3]
    outs = refs[blocks + 3 : 2 * blocks + 3]
    rows, total, combine, results = refs[2 * blocks + 3 :]
    expert, part = pl.program_id(0), pl.program_id(1)
    tok, model = outs[0].shape
    count = rows.shape[0]
    wide = count * cap

    @pl.when(jnp.logical_and(expert == 0, part == 0))
    def _():
        here = place[0] * count + lax.broadcasted_iota(jnp.int32, (LANES, wide), 1) // cap
        source = lax.broadcasted_iota(jnp.int32, (LANES, wide), 0)
        pick = jnp.where(jnp.logical_or(source == here, source == here + slots), 1.0, 0.0)
        pick = pick.astype(jnp.bfloat16)
        below = lax.broadcasted_iota(jnp.int32, (tok, tok), 0)
        across = lax.broadcasted_iota(jnp.int32, (tok, tok), 1)
        earlier = jnp.where(across < below, 1.0, 0.0).astype(jnp.bfloat16)
        slot = (lax.broadcasted_iota(jnp.int32, (tok, wide), 1) % cap).astype(jnp.float32)
        for b in range(blocks):
            weight = mm(x_refs[b][:, model : model + LANES], pick)
            chosen = weight > 0.0
            rank = mm(earlier, jnp.where(chosen, 1.0, 0.0).astype(jnp.bfloat16))
            match = jnp.logical_and(chosen, rank == slot)
            select = jnp.where(match, 1.0, 0.0).astype(jnp.bfloat16)
            picked = mm(select, x_refs[b][:, :model], TN).astype(jnp.bfloat16)
            for e in range(count):
                rows[e, b * cap : (b + 1) * cap, :] = picked[e * cap : (e + 1) * cap]
            weight = jnp.where(match, weight, 0.0)
            high = weight.astype(jnp.bfloat16)
            low = (weight - high.astype(jnp.float32)).astype(jnp.bfloat16)
            combine[b] = jnp.concatenate([high, low], axis=1)

    x = rows[expert]
    gate = mm(x, gate_ref[0])
    up = mm(x, up_ref[0])
    act = (gate / (1.0 + jnp.exp(-gate)) * up).astype(jnp.bfloat16)
    down = mm(act, down_ref[0])

    @pl.when(part == 0)
    def _():
        total[...] = down

    @pl.when(part > 0)
    def _():
        total[...] += down

    @pl.when(part == pl.num_programs(1) - 1)
    def _():
        for b in range(blocks):
            value = total[b * cap : (b + 1) * cap, :].astype(jnp.bfloat16)
            results[b, pl.ds(pl.multiple_of(expert * cap, cap), cap), :] = value
            results[b, pl.ds(pl.multiple_of(wide + expert * cap, cap), cap), :] = value

    @pl.when(jnp.logical_and(expert == count - 1, part == pl.num_programs(1) - 1))
    def _():
        for b in range(blocks):
            outs[b][...] = mm(combine[b], results[b]).astype(jnp.bfloat16)


def run_experts(xs, w_gate, w_up, w_down, place, cap, slots, parts):
    blocks = len(xs)
    tok, extended = xs[0].shape
    count, model, hidden = w_gate.shape
    tile = hidden // parts
    cost = pl.CostEstimate(
        flops=6 * count * blocks * cap * model * hidden,
        bytes_accessed=6 * count * model * hidden + 4 * blocks * tok * model,
        transcendentals=count * blocks * cap * hidden,
    )
    return pl.pallas_call(
        functools.partial(expert_kernel, blocks=blocks, cap=cap, slots=slots),
        out_shape=[jax.ShapeDtypeStruct((tok, model), jnp.bfloat16)] * blocks,
        grid_spec=pltpu.PrefetchScalarGridSpec(
            num_scalar_prefetch=1,
            grid=(count, parts),
            in_specs=[pl.BlockSpec((tok, extended), lambda e, f, place: (0, 0))] * blocks
            + [
                pl.BlockSpec((1, model, tile), lambda e, f, place: (e, 0, f)),
                pl.BlockSpec((1, model, tile), lambda e, f, place: (e, 0, f)),
                pl.BlockSpec((1, tile, model), lambda e, f, place: (e, f, 0)),
            ],
            out_specs=[pl.BlockSpec((tok, model), lambda e, f, place: (0, 0))] * blocks,
            scratch_shapes=[
                pltpu.VMEM((count, blocks * cap, model), jnp.bfloat16),
                pltpu.VMEM((blocks * cap, model), jnp.float32),
                pltpu.VMEM((blocks, tok, 2 * count * cap), jnp.bfloat16),
                pltpu.VMEM((blocks, 2 * count * cap, model), jnp.bfloat16),
            ],
        ),
        compiler_params=pltpu.CompilerParams(vmem_limit_bytes=40 * 1024 * 1024),
        cost_estimate=cost,
        name="experts",
    )(place, *xs, w_gate, w_up, w_down)


def add_low(a, b):
    return (a.astype(jnp.float32) + b.astype(jnp.float32)).astype(jnp.bfloat16)


def local(
    resid_in, head_in, gate_in, in_basis, out_basis, step_size, decay_rate, init_state, lengths,
    norm_gain, out_proj, moe_gain, expert_ids, route_weight, placement, w_gate, w_up, w_down,
):
    devices = lax.axis_size("mix")
    depth = devices // 4
    me = lax.axis_index("mix")
    place = me.astype(jnp.int32)[None]
    tokens = head_in.shape[0]
    tok = tokens // devices
    width = head_in.shape[1]

    def cross(x, mask):
        return lax.ppermute(x, "mix", [(i, i ^ mask) for i in range(devices)])

    def onward(x, stride=4):
        return lax.ppermute(x, "mix", [(i, (i + stride) % devices) for i in range(devices)])

    proj_y, proj_z = cross(out_proj, 2), cross(out_proj, 4)
    proj_yz = (cross(proj_y[: width // 2], 4), cross(proj_z[width // 2 :], 2))
    gains = jnp.take(norm_gain.reshape(devices, width), me ^ jnp.arange(8), axis=0)

    slots = placement.shape[0]
    slot_of = jnp.sum(
        jnp.where(
            expert_ids[:, :, None] == jnp.arange(slots, dtype=jnp.int32), placement[None, None, :], 0
        ),
        axis=2,
    )
    route = jnp.sum(
        jnp.where(
            slot_of[:, :, None] == jnp.arange(slots, dtype=jnp.int32), route_weight[:, :, None], 0.0
        ),
        axis=1,
    )
    route_high = lax.reduce_precision(route, 8, 7)
    table = jnp.concatenate([route_high, route - route_high], axis=1)
    table = jnp.pad(table, ((0, 0), (0, LANES - 2 * slots))).astype(jnp.bfloat16)

    gated = scan_heads(
        head_in, gate_in, in_basis, out_basis, step_size, decay_rate, init_state, lengths,
        place, depth // 2,
    )
    projs = []
    for block in (out_proj, proj_y, proj_z, *proj_yz):
        projs += [block, cross(block, 1)]
    acts = [gated[0]] + [cross(gated[mask], mask) for mask in range(1, 8)]
    halves = 2
    sums = []
    for half in range(halves):
        mixed, squares = project(gains, acts, projs, half, halves, half == 0)
        total = mixed[1]
        if half == 0:
            norm = squares[1]
        for dz in range(2, depth // 2):
            total = add_low(onward(total, 8), mixed[dz])
            if half == 0:
                norm = onward(norm, 8) + squares[dz]
        total = onward(total, 8).astype(jnp.float32) + mixed[0].astype(jnp.float32)
        if half == 0:
            norm = (onward(norm, 8) + squares[0])[:, 0:1]
        sums.append(total)
    mixer_sum = jnp.concatenate(sums, axis=1)
    hidden = resid_in.astype(jnp.float32) + mixer_sum * lax.rsqrt(norm / (devices * width) + epsilon)
    normed = (
        hidden * lax.rsqrt(jnp.mean(hidden * hidden, axis=1, keepdims=True) + epsilon) * moe_gain
    ).astype(jnp.bfloat16)
    mine = jnp.concatenate([normed, table], axis=1)

    cap = 2 * tok * expert_ids.shape[1] // slots
    sums = []
    for dz in range(depth):
        if dz > 0:
            mine = onward(mine)
        other = cross(mine, 2) if dz < depth - 1 else onward(other)
        block = [mine, cross(mine, 1), other, cross(other, 1)]
        outs = run_experts(block, w_gate, w_up, w_down, place, cap, slots, 1)
        near = add_low(outs[0], cross(outs[1], 1))
        far = add_low(outs[2], cross(outs[3], 1))
        sums.append(add_low(near, cross(far, 2)))
    total = sums[1]
    for dz in range(2, depth):
        total = add_low(onward(total), sums[dz])
    expert_sum = onward(total).astype(jnp.float32) + sums[0].astype(jnp.float32)
    return (hidden + expert_sum).astype(jnp.bfloat16)


def solution(mesh):
    return jax.shard_map(
        local,
        mesh=mesh,
        in_specs=(
            P(("groups", "mix"), None),
            P("groups", "mix"),
            P("groups", "mix"),
            P("groups", None),
            P("groups", None),
            P("mix", "groups"),
            P("mix"),
            P("groups", "mix", None, None),
            P("groups"),
            P(),
            P("mix", None),
            P(),
            P(("groups", "mix"), None),
            P(("groups", "mix"), None),
            P(),
            P("mix", None, None),
            P("mix", None, None),
            P("mix", None, None),
        ),
        out_specs=P(("groups", "mix"), None),
        check_vma=False,
    )
```

```python
import functools

import jax
import jax.numpy as jnp
from jax import lax
from jax.experimental import pallas as pl
from jax.experimental.pallas import tpu as pltpu
from jax.sharding import PartitionSpec as P


epsilon = 1e-05
LANES = 128
NT = (((1,), (1,)), ((), ()))
TN = (((0,), (0,)), ((), ()))


def mm(a, b, dims=(((1,), (0,)), ((), ())), precision=None):
    return lax.dot_general(
        a, b, dims, precision=precision, preferred_element_type=jnp.float32
    )


def scan_kernel(
    lengths, place, rates, step_ref, x_ref, g_ref, b_ref, c_ref, init_ref, *refs, span, chunks
):
    out_refs, (runs, rows, state, src, first_src) = refs[:8], refs[8:]
    heads, tokens = step_ref.shape
    requests, width, _ = init_ref.shape
    tok = out_refs[0].shape[1]
    head_dim = width // heads
    starts = [jnp.int32(0)]
    for r in range(requests - 1):
        starts.append(starts[-1] + lengths[r])

    @pl.when(pl.program_id(0) == 0)
    def _():
        state[...] = jnp.zeros_like(state)
        runs[...] = jnp.zeros_like(runs)
        for h in range(heads):
            runs[h : h + 1, :] = -step_ref[h : h + 1, :] * rates[h]
        run = runs[...]
        lane = lax.broadcasted_iota(jnp.int32, run.shape, 1)
        inner = lane % span
        shift = 1
        while shift < span:
            run = run + jnp.where(inner >= shift, pltpu.roll(run, shift, 1), 0.0)
            shift *= 2
        runs[...] = run
        final = lane - inner + (span - 1)
        before = jnp.zeros_like(run)
        first_last = jnp.zeros_like(lane)
        for start in starts:
            end = start - start % span + span
            inside = jnp.logical_and(lane == start - 1, start % span > 0)
            value = jnp.sum(jnp.where(inside, run, 0.0), axis=1, keepdims=True)
            before = jnp.where(jnp.logical_and(lane >= start, lane < end), value, before)
            first_last = jnp.where(final >= start, start, first_last)
        weight = jnp.exp(run - before)
        ends = [
            jnp.broadcast_to(run[:, at + span - 1 : at + span], (8, span))
            for at in range(0, tokens, span)
        ]
        ends = jnp.concatenate(ends, axis=1)
        last = jnp.where(lane >= first_last, jnp.exp(ends - run), 0.0)
        zeros = jnp.zeros_like(run)
        steps = jnp.concatenate([step_ref[...], zeros[heads:]], axis=0)
        for i, value in enumerate((steps, last, weight)):
            high = value.astype(jnp.bfloat16)
            low = (value - high.astype(jnp.float32)).astype(jnp.bfloat16)
            rows[16 * i : 16 * i + 16, :] = jnp.concatenate([high, low], axis=0)

    spread_row = lax.broadcasted_iota(jnp.int32, (48, 3 * width), 0)
    spread_col = lax.broadcasted_iota(jnp.int32, (48, 3 * width), 1)
    spread = jnp.logical_and(
        spread_row // 16 == spread_col // width, spread_row % 8 == spread_col % width // head_dim
    )
    spread = jnp.where(spread, 1.0, 0.0).astype(jnp.bfloat16)
    row = lax.broadcasted_iota(jnp.int32, (span, span), 0)
    col = lax.broadcasted_iota(jnp.int32, (span, span), 1)
    causal = col <= row
    per_tile = LANES // head_dim
    tile_lane = lax.broadcasted_iota(jnp.int32, (span, LANES), 1) // head_dim
    local_pos = lax.broadcasted_iota(jnp.int32, (span, 1), 0)

    for u in range(chunks):
        chunk = pl.program_id(0) * chunks + u
        c0 = pl.multiple_of(chunk * span, span)
        here = pl.ds(u * span, span)
        run = runs[:, pl.ds(c0, span)]
        pos = local_pos + c0
        first = jnp.zeros_like(pos)
        for start in starts:
            first = jnp.where(pos >= start, start, first)
        spread_all = mm(rows[:, pl.ds(c0, span)], spread, TN)
        weight_wide = spread_all[:, 2 * width :]
        drive = x_ref[here, :].astype(jnp.float32) * spread_all[:, :width]
        drive_low = drive.astype(jnp.bfloat16)
        drive_last = (drive * spread_all[:, width : 2 * width]).astype(jnp.bfloat16)
        basis = b_ref[here, :]
        readout = c_ref[here, :]
        valid = jnp.logical_and(causal, col >= first - c0)
        scores = jnp.where(valid, mm(readout, basis, NT), 0.0)

        src[...] = mm(readout, state[...].astype(jnp.bfloat16))
        first_src[...] = state[...]
        for r, start in enumerate(starts):

            @pl.when(jnp.logical_and(start >= c0, start < c0 + span))
            def _(r=r, start=start):
                init = init_ref[r].T
                mine = mm(readout, init.astype(jnp.bfloat16))
                src[...] = jnp.where(first == start, mine, src[...])
                first_src[...] = init

        run_cols = run.T
        pieces = []
        for tile in range(heads // per_tile):
            drive_tile = drive_low[:, tile * LANES : (tile + 1) * LANES]
            piece = None
            for j in range(per_tile):
                h = tile * per_tile + j
                gap = jnp.minimum(run_cols[:, h : h + 1] - run[h : h + 1, :], 0.0)
                part = mm((jnp.exp(gap) * scores).astype(jnp.bfloat16), drive_tile)
                piece = part if piece is None else jnp.where(tile_lane == j, part, piece)
            pieces.append(piece)
        within = pieces[0] if len(pieces) == 1 else jnp.concatenate(pieces, axis=1)
        output = within + weight_wide * src[...]
        state[...] = mm(basis, drive_last, TN) + weight_wide[span - 1 : span, :] * first_src[...]
        gate = g_ref[here, :].astype(jnp.float32)
        gated = (output * (gate / (1.0 + jnp.exp(-gate)))).astype(jnp.bfloat16)
        even = lax.rem(place[0], 2) == 0
        mine = jnp.where(even, gated[:tok], gated[tok:])
        other = jnp.where(even, gated[tok:], gated[:tok])
        pair = lax.rem(chunk, 4) ^ lax.div(lax.rem(place[0], 8), 2)
        for way in range(4):

            @pl.when(pair == way)
            def _(way=way, mine=mine, other=other):
                out_refs[2 * way][0] = mine
                out_refs[2 * way + 1][0] = other


def scan_heads(head_in, gate_in, in_basis, out_basis, step, rate, init, lengths, place, depth):
    tokens, width = head_in.shape
    heads = step.shape[0]
    requests = lengths.shape[0]
    states = in_basis.shape[1]
    tok = tokens // (8 * depth)
    span = 2 * tok
    chunks = 2
    block = chunks * span
    init = init.reshape(requests, width, states)
    cost = pl.CostEstimate(
        flops=2 * tokens * width * (span * 2 + 3 * states),
        bytes_accessed=6 * tokens * width,
        transcendentals=tokens * span * heads,
    )

    def row_block(i, lengths, place, rates):
        return (i, 0)

    def out_block(i, lengths, place, rates):
        return (lax.rem(lax.div(place[0], 8) - lax.div(i * chunks, 4) + depth, depth), 0, 0)

    return pl.pallas_call(
        functools.partial(scan_kernel, span=span, chunks=chunks),
        out_shape=[jax.ShapeDtypeStruct((depth, tok, width), jnp.bfloat16)] * 8,
        grid_spec=pltpu.PrefetchScalarGridSpec(
            num_scalar_prefetch=3,
            grid=(tokens // block,),
            in_specs=[
                pl.BlockSpec((heads, tokens), lambda i, lengths, place, rates: (0, 0)),
                pl.BlockSpec((block, width), row_block),
                pl.BlockSpec((block, width), row_block),
                pl.BlockSpec((block, states), row_block),
                pl.BlockSpec((block, states), row_block),
                pl.BlockSpec((requests, width, states), lambda i, lengths, place, rates: (0, 0, 0)),
            ],
            out_specs=[pl.BlockSpec((1, tok, width), out_block)] * 8,
            scratch_shapes=[
                pltpu.VMEM((8, tokens), jnp.float32),
                pltpu.VMEM((48, tokens), jnp.bfloat16),
                pltpu.VMEM((states, width), jnp.float32),
                pltpu.VMEM((span, width), jnp.float32),
                pltpu.VMEM((states, width), jnp.float32),
            ],
        ),
        cost_estimate=cost,
        name="scan",
    )(lengths, place, rate, step, head_in, gate_in, in_basis, out_basis, init)


def project_kernel(*refs, depth, squared):
    gain_ref, acts, refs = refs[0], refs[1:9], refs[9:]
    weights, refs = refs[:10], refs[10:]
    outs, squares = refs[:depth], refs[depth:]
    _, tok, width = acts[0].shape
    total = None
    for mask, act in enumerate(acts):
        rows = act[...].reshape(depth * tok, width).astype(jnp.float32)
        rows = (rows * gain_ref[mask : mask + 1, :]).astype(jnp.bfloat16)
        if mask < 6:
            part = mm(rows, weights[mask][...])
        else:
            halves = weights[6 + mask % 2], weights[8 + mask % 2]
            part = mm(rows, jnp.concatenate([h[...] for h in halves], axis=0))
        total = part if total is None else total + part
    for dz in range(depth):
        outs[dz][...] = total[dz * tok : (dz + 1) * tok].astype(jnp.bfloat16)
    if squared:

        @pl.when(pl.program_id(0) == 0)
        def _():
            for dz in range(depth):
                wide = [act[dz].astype(jnp.float32) for act in acts]
                summed = sum(jnp.sum(w * w, axis=1, keepdims=True) for w in wide)
                squares[dz][...] = jnp.broadcast_to(summed, (tok, LANES))


def project(gains, acts, weights, half, halves, squared):
    depth, tok, width = acts[0].shape
    model = weights[0].shape[1]
    steps = 2
    columns = model // halves // steps
    cost = pl.CostEstimate(
        flops=16 * depth * tok * width * model // halves,
        bytes_accessed=2 * (8 * width * model + depth * tok * (model + 8 * width)) // halves,
        transcendentals=0,
    )
    out_shape = [jax.ShapeDtypeStruct((tok, columns * steps), jnp.bfloat16)] * depth
    out_specs = [pl.BlockSpec((tok, columns), lambda i: (0, i))] * depth
    if squared:
        out_shape += [jax.ShapeDtypeStruct((tok, LANES), jnp.float32)] * depth
        out_specs += [pl.BlockSpec((tok, LANES), lambda i: (0, 0))] * depth
    out = pl.pallas_call(
        functools.partial(project_kernel, depth=depth, squared=squared),
        out_shape=out_shape,
        grid=(steps,),
        in_specs=[pl.BlockSpec((8, width), lambda i: (0, 0))]
        + [pl.BlockSpec((depth, tok, width), lambda i: (0, 0, 0))] * 8
        + [pl.BlockSpec((w.shape[0], columns), lambda i: (0, half * steps + i)) for w in weights],
        out_specs=out_specs,
        cost_estimate=cost,
        name="project",
    )(gains, *acts, *weights)
    return out[:depth], out[depth:]


def expert_kernel(place, *refs, blocks, cap, slots):
    firsts, seconds, refs = refs[:blocks], refs[blocks : 2 * blocks], refs[2 * blocks :]
    gate_ref, up_ref, down_ref = refs[:3]
    outs = refs[3 : blocks + 3]
    rows, total, combine, results = refs[blocks + 3 :]
    expert, part = pl.program_id(0), pl.program_id(1)
    tok, model = outs[0].shape
    half = model // 2
    count = rows.shape[0]
    wide = count * cap

    @pl.when(jnp.logical_and(expert == 0, part == 0))
    def _():
        here = place[0] * count + lax.broadcasted_iota(jnp.int32, (LANES, wide), 1) // cap
        source = lax.broadcasted_iota(jnp.int32, (LANES, wide), 0)
        pick = jnp.where(jnp.logical_or(source == here, source == here + slots), 1.0, 0.0)
        pick = pick.astype(jnp.bfloat16)
        below = lax.broadcasted_iota(jnp.int32, (tok, tok), 0)
        across = lax.broadcasted_iota(jnp.int32, (tok, tok), 1)
        earlier = jnp.where(across < below, 1.0, 0.0).astype(jnp.bfloat16)
        slot = (lax.broadcasted_iota(jnp.int32, (tok, wide), 1) % cap).astype(jnp.float32)
        for b in range(blocks):
            weight = mm(seconds[b][:, half : half + LANES], pick)
            chosen = weight > 0.0
            rank = mm(earlier, jnp.where(chosen, 1.0, 0.0).astype(jnp.bfloat16))
            match = jnp.logical_and(chosen, rank == slot)
            select = jnp.where(match, 1.0, 0.0).astype(jnp.bfloat16)
            for at, ref in ((0, firsts[b]), (half, seconds[b])):
                picked = mm(select, ref[:, :half], TN).astype(jnp.bfloat16)
                for e in range(count):
                    rows[e, b * cap : (b + 1) * cap, at : at + half] = picked[e * cap : (e + 1) * cap]
            weight = jnp.where(match, weight, 0.0)
            high = weight.astype(jnp.bfloat16)
            low = (weight - high.astype(jnp.float32)).astype(jnp.bfloat16)
            combine[b] = jnp.concatenate([high, low], axis=1)

    x = rows[expert]
    gate = mm(x, gate_ref[0])
    up = mm(x, up_ref[0])
    act = (gate / (1.0 + jnp.exp(-gate)) * up).astype(jnp.bfloat16)
    down = mm(act, down_ref[0])

    @pl.when(part == 0)
    def _():
        total[...] = down

    @pl.when(part > 0)
    def _():
        total[...] += down

    @pl.when(part == pl.num_programs(1) - 1)
    def _():
        for b in range(blocks):
            value = total[b * cap : (b + 1) * cap, :].astype(jnp.bfloat16)
            results[b, pl.ds(pl.multiple_of(expert * cap, cap), cap), :] = value
            results[b, pl.ds(pl.multiple_of(wide + expert * cap, cap), cap), :] = value

    @pl.when(jnp.logical_and(expert == count - 1, part == pl.num_programs(1) - 1))
    def _():
        for b in range(blocks):
            outs[b][...] = mm(combine[b], results[b]).astype(jnp.bfloat16)


def run_experts(xs, w_gate, w_up, w_down, place, cap, slots, parts):
    blocks = len(xs) // 2
    tok = xs[0].shape[0]
    count, model, hidden = w_gate.shape
    tile = hidden // parts
    cost = pl.CostEstimate(
        flops=6 * count * blocks * cap * model * hidden,
        bytes_accessed=6 * count * model * hidden + 4 * blocks * tok * model,
        transcendentals=count * blocks * cap * hidden,
    )
    return pl.pallas_call(
        functools.partial(expert_kernel, blocks=blocks, cap=cap, slots=slots),
        out_shape=[jax.ShapeDtypeStruct((tok, model), jnp.bfloat16)] * blocks,
        grid_spec=pltpu.PrefetchScalarGridSpec(
            num_scalar_prefetch=1,
            grid=(count, parts),
            in_specs=[pl.BlockSpec(x.shape, lambda e, f, place: (0, 0)) for x in xs]
            + [
                pl.BlockSpec((1, model, tile), lambda e, f, place: (e, 0, f)),
                pl.BlockSpec((1, model, tile), lambda e, f, place: (e, 0, f)),
                pl.BlockSpec((1, tile, model), lambda e, f, place: (e, f, 0)),
            ],
            out_specs=[pl.BlockSpec((tok, model), lambda e, f, place: (0, 0))] * blocks,
            scratch_shapes=[
                pltpu.VMEM((count, blocks * cap, model), jnp.bfloat16),
                pltpu.VMEM((blocks * cap, model), jnp.float32),
                pltpu.VMEM((blocks, tok, 2 * count * cap), jnp.bfloat16),
                pltpu.VMEM((blocks, 2 * count * cap, model), jnp.bfloat16),
            ],
        ),
        compiler_params=pltpu.CompilerParams(vmem_limit_bytes=46 * 1024 * 1024),
        cost_estimate=cost,
        name="experts",
    )(place, *xs, w_gate, w_up, w_down)


def add_low(a, b):
    return (a.astype(jnp.float32) + b.astype(jnp.float32)).astype(jnp.bfloat16)


def local(
    resid_in, head_in, gate_in, in_basis, out_basis, step_size, decay_rate, init_state, lengths,
    norm_gain, out_proj, moe_gain, expert_ids, route_weight, placement, w_gate, w_up, w_down,
):
    devices = lax.axis_size("mix")
    depth = devices // 4
    me = lax.axis_index("mix")
    place = me.astype(jnp.int32)[None]
    tokens = head_in.shape[0]
    tok = tokens // devices
    width = head_in.shape[1]
    model = out_proj.shape[1]

    def cross(x, mask):
        return lax.ppermute(x, "mix", [(i, i ^ mask) for i in range(devices)])

    def onward(x, stride=4):
        return lax.ppermute(x, "mix", [(i, (i + stride) % devices) for i in range(devices)])

    proj_y, proj_z = cross(out_proj, 2), cross(out_proj, 4)
    proj_yz = (cross(proj_y[: width // 2], 4), cross(proj_z[width // 2 :], 2))
    gains = jnp.take(norm_gain.reshape(devices, width), me ^ jnp.arange(8), axis=0)

    slots = placement.shape[0]
    slot_of = jnp.sum(
        jnp.where(
            expert_ids[:, :, None] == jnp.arange(slots, dtype=jnp.int32), placement[None, None, :], 0
        ),
        axis=2,
    )
    route = jnp.sum(
        jnp.where(
            slot_of[:, :, None] == jnp.arange(slots, dtype=jnp.int32), route_weight[:, :, None], 0.0
        ),
        axis=1,
    )
    route_high = lax.reduce_precision(route, 8, 7)
    table = jnp.concatenate([route_high, route - route_high], axis=1)
    table = jnp.pad(table, ((0, 0), (0, LANES - 2 * slots))).astype(jnp.bfloat16)

    gated = scan_heads(
        head_in, gate_in, in_basis, out_basis, step_size, decay_rate, init_state, lengths,
        place, depth // 2,
    )
    projs = []
    for block in (out_proj, proj_y, proj_z, *proj_yz):
        projs += [block, cross(block, 1)]
    acts = [gated[0]] + [cross(gated[mask], mask) for mask in range(1, 8)]
    halves = 2
    sums = []
    for half in range(halves):
        mixed, squares = project(gains, acts, projs, half, halves, half == 0)
        total = mixed[1]
        if half == 0:
            norm = squares[1]
        for dz in range(2, depth // 2):
            total = add_low(onward(total, 8), mixed[dz])
            if half == 0:
                norm = onward(norm, 8) + squares[dz]
        total = onward(total, 8).astype(jnp.float32) + mixed[0].astype(jnp.float32)
        if half == 0:
            norm = (onward(norm, 8) + squares[0])[:, 0:1]
        sums.append(total)
    mixer_sum = jnp.concatenate(sums, axis=1)
    hidden = resid_in.astype(jnp.float32) + mixer_sum * lax.rsqrt(norm / (devices * width) + epsilon)
    normed = (
        hidden * lax.rsqrt(jnp.mean(hidden * hidden, axis=1, keepdims=True) + epsilon) * moe_gain
    ).astype(jnp.bfloat16)
    mine = [normed[:, : model // 2], jnp.concatenate([normed[:, model // 2 :], table], axis=1)]

    cap = 2 * tok * expert_ids.shape[1] // slots
    both = (0, 1)
    cut = model // 2 + LANES
    sides = (slice(0, cut), slice(cut, model))
    sums = []
    for dz in range(depth):
        if dz > 0:
            mine = [onward(mine[h]) for h in both]
        if dz < depth - 1:
            other = [cross(mine[h], 2) for h in both]
        else:
            other = [onward(other[h]) for h in both]
        block = []
        for h in both:
            block += [mine[h], cross(mine[h], 1)]
            block += [other[h], cross(other[h], 1)]
        outs = run_experts(block, w_gate, w_up, w_down, place, cap, slots, 1)
        near_c, far_c = cross(outs[1], 1), cross(outs[3], 1)
        parts = []
        for h in both:
            columns = sides[h]
            near = add_low(outs[0][:, columns], near_c[:, columns])
            far = add_low(outs[2][:, columns], far_c[:, columns])
            far = cross(far, 2)
            parts.append(add_low(near, far))
        sums.append(parts)
    results = []
    for h in both:
        total = sums[1][h]
        for dz in range(2, depth):
            total = onward(total)
            total = add_low(total, sums[dz][h])
        expert_sum = onward(total).astype(jnp.float32) + sums[0][h].astype(jnp.float32)
        results.append(hidden[:, sides[h]] + expert_sum)
    return jnp.concatenate(results, axis=1).astype(jnp.bfloat16)


def solution(mesh):
    return jax.shard_map(
        local,
        mesh=mesh,
        in_specs=(
            P(("groups", "mix"), None),
            P("groups", "mix"),
            P("groups", "mix"),
            P("groups", None),
            P("groups", None),
            P("mix", "groups"),
            P("mix"),
            P("groups", "mix", None, None),
            P("groups"),
            P(),
            P("mix", None),
            P(),
            P(("groups", "mix"), None),
            P(("groups", "mix"), None),
            P(),
            P("mix", None, None),
            P("mix", None, None),
            P("mix", None, None),
        ),
        out_specs=P(("groups", "mix"), None),
        check_vma=False,
    )
```

```python
import functools

import jax
import jax.numpy as jnp
from jax import lax
from jax.experimental import pallas as pl
from jax.experimental.pallas import tpu as pltpu
from jax.sharding import PartitionSpec as P


epsilon = 1e-05
LANES = 128
NT = (((1,), (1,)), ((), ()))
TN = (((0,), (0,)), ((), ()))


def mm(a, b, dims=(((1,), (0,)), ((), ())), precision=None):
    return lax.dot_general(
        a, b, dims, precision=precision, preferred_element_type=jnp.float32
    )


def scan_kernel(
    lengths, place, rates, step_ref, x_ref, g_ref, b_ref, c_ref, init_ref, *refs, span, chunks
):
    out_refs, (runs, rows, state, src, first_src) = refs[:8], refs[8:]
    heads, tokens = step_ref.shape
    requests, width, _ = init_ref.shape
    tok = out_refs[0].shape[1]
    head_dim = width // heads
    starts = [jnp.int32(0)]
    for r in range(requests - 1):
        starts.append(starts[-1] + lengths[r])

    @pl.when(pl.program_id(0) == 0)
    def _():
        state[...] = jnp.zeros_like(state)
        runs[...] = jnp.zeros_like(runs)
        for h in range(heads):
            runs[h : h + 1, :] = -step_ref[h : h + 1, :] * rates[h]
        run = runs[...]
        lane = lax.broadcasted_iota(jnp.int32, run.shape, 1)
        inner = lane % span
        shift = 1
        while shift < span:
            run = run + jnp.where(inner >= shift, pltpu.roll(run, shift, 1), 0.0)
            shift *= 2
        runs[...] = run
        final = lane - inner + (span - 1)
        before = jnp.zeros_like(run)
        first_last = jnp.zeros_like(lane)
        for start in starts:
            end = start - start % span + span
            inside = jnp.logical_and(lane == start - 1, start % span > 0)
            value = jnp.sum(jnp.where(inside, run, 0.0), axis=1, keepdims=True)
            before = jnp.where(jnp.logical_and(lane >= start, lane < end), value, before)
            first_last = jnp.where(final >= start, start, first_last)
        weight = jnp.exp(run - before)
        ends = [
            jnp.broadcast_to(run[:, at + span - 1 : at + span], (8, span))
            for at in range(0, tokens, span)
        ]
        ends = jnp.concatenate(ends, axis=1)
        last = jnp.where(lane >= first_last, jnp.exp(ends - run), 0.0)
        zeros = jnp.zeros_like(run)
        steps = jnp.concatenate([step_ref[...], zeros[heads:]], axis=0)
        for i, value in enumerate((steps, last, weight)):
            high = value.astype(jnp.bfloat16)
            low = (value - high.astype(jnp.float32)).astype(jnp.bfloat16)
            rows[16 * i : 16 * i + 16, :] = jnp.concatenate([high, low], axis=0)

    spread_row = lax.broadcasted_iota(jnp.int32, (48, 3 * width), 0)
    spread_col = lax.broadcasted_iota(jnp.int32, (48, 3 * width), 1)
    spread = jnp.logical_and(
        spread_row // 16 == spread_col // width, spread_row % 8 == spread_col % width // head_dim
    )
    spread = jnp.where(spread, 1.0, 0.0).astype(jnp.bfloat16)
    row = lax.broadcasted_iota(jnp.int32, (span, span), 0)
    col = lax.broadcasted_iota(jnp.int32, (span, span), 1)
    causal = col <= row
    per_tile = LANES // head_dim
    tile_lane = lax.broadcasted_iota(jnp.int32, (span, LANES), 1) // head_dim
    local_pos = lax.broadcasted_iota(jnp.int32, (span, 1), 0)

    for u in range(chunks):
        chunk = pl.program_id(0) * chunks + u
        c0 = pl.multiple_of(chunk * span, span)
        here = pl.ds(u * span, span)
        run = runs[:, pl.ds(c0, span)]
        pos = local_pos + c0
        first = jnp.zeros_like(pos)
        for start in starts:
            first = jnp.where(pos >= start, start, first)
        spread_all = mm(rows[:, pl.ds(c0, span)], spread, TN)
        weight_wide = spread_all[:, 2 * width :]
        drive = x_ref[here, :].astype(jnp.float32) * spread_all[:, :width]
        drive_low = drive.astype(jnp.bfloat16)
        drive_last = (drive * spread_all[:, width : 2 * width]).astype(jnp.bfloat16)
        basis = b_ref[here, :]
        readout = c_ref[here, :]
        valid = jnp.logical_and(causal, col >= first - c0)
        scores = jnp.where(valid, mm(readout, basis, NT), 0.0)

        src[...] = mm(readout, state[...].astype(jnp.bfloat16))
        first_src[...] = state[...]
        for r, start in enumerate(starts):

            @pl.when(jnp.logical_and(start >= c0, start < c0 + span))
            def _(r=r, start=start):
                init = init_ref[r].T
                mine = mm(readout, init.astype(jnp.bfloat16))
                src[...] = jnp.where(first == start, mine, src[...])
                first_src[...] = init

        run_cols = run.T
        pieces = []
        for tile in range(heads // per_tile):
            drive_tile = drive_low[:, tile * LANES : (tile + 1) * LANES]
            piece = None
            for j in range(per_tile):
                h = tile * per_tile + j
                gap = jnp.minimum(run_cols[:, h : h + 1] - run[h : h + 1, :], 0.0)
                part = mm((jnp.exp(gap) * scores).astype(jnp.bfloat16), drive_tile)
                piece = part if piece is None else jnp.where(tile_lane == j, part, piece)
            pieces.append(piece)
        within = pieces[0] if len(pieces) == 1 else jnp.concatenate(pieces, axis=1)
        output = within + weight_wide * src[...]
        state[...] = mm(basis, drive_last, TN) + weight_wide[span - 1 : span, :] * first_src[...]
        gate = g_ref[here, :].astype(jnp.float32)
        gated = (output * (gate / (1.0 + jnp.exp(-gate)))).astype(jnp.bfloat16)
        even = lax.rem(place[0], 2) == 0
        mine = jnp.where(even, gated[:tok], gated[tok:])
        other = jnp.where(even, gated[tok:], gated[:tok])
        pair = lax.rem(chunk, 4) ^ lax.div(lax.rem(place[0], 8), 2)
        for way in range(4):

            @pl.when(pair == way)
            def _(way=way, mine=mine, other=other):
                out_refs[2 * way][0] = mine
                out_refs[2 * way + 1][0] = other


def scan_heads(head_in, gate_in, in_basis, out_basis, step, rate, init, lengths, place, depth):
    tokens, width = head_in.shape
    heads = step.shape[0]
    requests = lengths.shape[0]
    states = in_basis.shape[1]
    tok = tokens // (8 * depth)
    span = 2 * tok
    chunks = 2
    block = chunks * span
    init = init.reshape(requests, width, states)
    cost = pl.CostEstimate(
        flops=2 * tokens * width * (span * 2 + 3 * states),
        bytes_accessed=6 * tokens * width,
        transcendentals=tokens * span * heads,
    )

    def row_block(i, lengths, place, rates):
        return (i, 0)

    def out_block(i, lengths, place, rates):
        return (lax.rem(lax.div(place[0], 8) - lax.div(i * chunks, 4) + depth, depth), 0, 0)

    return pl.pallas_call(
        functools.partial(scan_kernel, span=span, chunks=chunks),
        out_shape=[jax.ShapeDtypeStruct((depth, tok, width), jnp.bfloat16)] * 8,
        grid_spec=pltpu.PrefetchScalarGridSpec(
            num_scalar_prefetch=3,
            grid=(tokens // block,),
            in_specs=[
                pl.BlockSpec((heads, tokens), lambda i, lengths, place, rates: (0, 0)),
                pl.BlockSpec((block, width), row_block),
                pl.BlockSpec((block, width), row_block),
                pl.BlockSpec((block, states), row_block),
                pl.BlockSpec((block, states), row_block),
                pl.BlockSpec((requests, width, states), lambda i, lengths, place, rates: (0, 0, 0)),
            ],
            out_specs=[pl.BlockSpec((1, tok, width), out_block)] * 8,
            scratch_shapes=[
                pltpu.VMEM((8, tokens), jnp.float32),
                pltpu.VMEM((48, tokens), jnp.bfloat16),
                pltpu.VMEM((states, width), jnp.float32),
                pltpu.VMEM((span, width), jnp.float32),
                pltpu.VMEM((states, width), jnp.float32),
            ],
        ),
        cost_estimate=cost,
        name="scan",
    )(lengths, place, rate, step, head_in, gate_in, in_basis, out_basis, init)


def project_kernel(*refs, depth, squared):
    gain_ref, acts, refs = refs[0], refs[1:9], refs[9:]
    weights, refs = refs[:8], refs[8:]
    outs, squares = refs[:depth], refs[depth:]
    _, tok, width = acts[0].shape
    total = None
    for mask, act in enumerate(acts):
        rows = act[...].reshape(depth * tok, width).astype(jnp.float32)
        rows = (rows * gain_ref[mask : mask + 1, :]).astype(jnp.bfloat16)
        part = mm(rows, weights[mask][...])
        total = part if total is None else total + part
    for dz in range(depth):
        outs[dz][...] = total[dz * tok : (dz + 1) * tok].astype(jnp.bfloat16)
    if squared:

        @pl.when(pl.program_id(0) == 0)
        def _():
            for dz in range(depth):
                wide = [act[dz].astype(jnp.float32) for act in acts]
                summed = sum(jnp.sum(w * w, axis=1, keepdims=True) for w in wide)
                squares[dz][...] = jnp.broadcast_to(summed, (tok, LANES))


def project(gains, acts, weights, start, steps, columns, squared):
    depth, tok, width = acts[0].shape
    part = steps * columns
    cost = pl.CostEstimate(
        flops=16 * depth * tok * width * part,
        bytes_accessed=2 * (8 * width * part + depth * tok * (part + 8 * width)),
        transcendentals=0,
    )
    out_shape = [jax.ShapeDtypeStruct((tok, columns * steps), jnp.bfloat16)] * depth
    out_specs = [pl.BlockSpec((tok, columns), lambda i: (0, i))] * depth
    if squared:
        out_shape += [jax.ShapeDtypeStruct((tok, LANES), jnp.float32)] * depth
        out_specs += [pl.BlockSpec((tok, LANES), lambda i: (0, 0))] * depth
    out = pl.pallas_call(
        functools.partial(project_kernel, depth=depth, squared=squared),
        out_shape=out_shape,
        grid=(steps,),
        in_specs=[pl.BlockSpec((8, width), lambda i: (0, 0))]
        + [pl.BlockSpec((depth, tok, width), lambda i: (0, 0, 0))] * 8
        + [pl.BlockSpec((w.shape[0], columns), lambda i: (0, start + i)) for w in weights],
        out_specs=out_specs,
        cost_estimate=cost,
        name="project",
    )(gains, *acts, *weights)
    return out[:depth], out[depth:]


def expert_kernel(place, *refs, blocks, cap, slots):
    x_refs = refs[:blocks]
    gate_ref, up_ref, down_ref = refs[blocks : blocks + 3]
    outs = refs[blocks + 3 : 2 * blocks + 3]
    rows, total, combine, results = refs[2 * blocks + 3 :]
    expert, part = pl.program_id(0), pl.program_id(1)
    tok, model = outs[0].shape
    count = rows.shape[0]
    wide = count * cap

    @pl.when(jnp.logical_and(expert == 0, part == 0))
    def _():
        here = place[0] * count + lax.broadcasted_iota(jnp.int32, (LANES, wide), 1) // cap
        source = lax.broadcasted_iota(jnp.int32, (LANES, wide), 0)
        pick = jnp.where(jnp.logical_or(source == here, source == here + slots), 1.0, 0.0)
        pick = pick.astype(jnp.bfloat16)
        below = lax.broadcasted_iota(jnp.int32, (tok, tok), 0)
        across = lax.broadcasted_iota(jnp.int32, (tok, tok), 1)
        earlier = jnp.where(across < below, 1.0, 0.0).astype(jnp.bfloat16)
        slot = (lax.broadcasted_iota(jnp.int32, (tok, wide), 1) % cap).astype(jnp.float32)
        for b in range(blocks):
            weight = mm(x_refs[b][:, model : model + LANES], pick)
            chosen = weight > 0.0
            rank = mm(earlier, jnp.where(chosen, 1.0, 0.0).astype(jnp.bfloat16))
            match = jnp.logical_and(chosen, rank == slot)
            select = jnp.where(match, 1.0, 0.0).astype(jnp.bfloat16)
            picked = mm(select, x_refs[b][:, :model], TN).astype(jnp.bfloat16)
            for e in range(count):
                rows[e, b * cap : (b + 1) * cap, :] = picked[e * cap : (e + 1) * cap]
            weight = jnp.where(match, weight, 0.0)
            high = weight.astype(jnp.bfloat16)
            low = (weight - high.astype(jnp.float32)).astype(jnp.bfloat16)
            combine[b] = jnp.concatenate([high, low], axis=1)

    x = rows[expert]
    gate = mm(x, gate_ref[0])
    up = mm(x, up_ref[0])
    act = (gate / (1.0 + jnp.exp(-gate)) * up).astype(jnp.bfloat16)
    down = mm(act, down_ref[0])

    @pl.when(part == 0)
    def _():
        total[...] = down

    @pl.when(part > 0)
    def _():
        total[...] += down

    @pl.when(part == pl.num_programs(1) - 1)
    def _():
        for b in range(blocks):
            value = total[b * cap : (b + 1) * cap, :].astype(jnp.bfloat16)
            results[b, pl.ds(pl.multiple_of(expert * cap, cap), cap), :] = value
            results[b, pl.ds(pl.multiple_of(wide + expert * cap, cap), cap), :] = value

    @pl.when(jnp.logical_and(expert == count - 1, part == pl.num_programs(1) - 1))
    def _():
        for b in range(blocks):
            outs[b][...] = mm(combine[b], results[b]).astype(jnp.bfloat16)


def run_experts(xs, w_gate, w_up, w_down, place, cap, slots, parts):
    blocks = len(xs)
    tok, extended = xs[0].shape
    count, model, hidden = w_gate.shape
    tile = hidden // parts
    cost = pl.CostEstimate(
        flops=6 * count * blocks * cap * model * hidden,
        bytes_accessed=6 * count * model * hidden + 4 * blocks * tok * model,
        transcendentals=count * blocks * cap * hidden,
    )
    return pl.pallas_call(
        functools.partial(expert_kernel, blocks=blocks, cap=cap, slots=slots),
        out_shape=[jax.ShapeDtypeStruct((tok, model), jnp.bfloat16)] * blocks,
        grid_spec=pltpu.PrefetchScalarGridSpec(
            num_scalar_prefetch=1,
            grid=(count, parts),
            in_specs=[pl.BlockSpec((tok, extended), lambda e, f, place: (0, 0))] * blocks
            + [
                pl.BlockSpec((1, model, tile), lambda e, f, place: (e, 0, f)),
                pl.BlockSpec((1, model, tile), lambda e, f, place: (e, 0, f)),
                pl.BlockSpec((1, tile, model), lambda e, f, place: (e, f, 0)),
            ],
            out_specs=[pl.BlockSpec((tok, model), lambda e, f, place: (0, 0))] * blocks,
            scratch_shapes=[
                pltpu.VMEM((count, blocks * cap, model), jnp.bfloat16),
                pltpu.VMEM((blocks * cap, model), jnp.float32),
                pltpu.VMEM((blocks, tok, 2 * count * cap), jnp.bfloat16),
                pltpu.VMEM((blocks, 2 * count * cap, model), jnp.bfloat16),
            ],
        ),
        compiler_params=pltpu.CompilerParams(vmem_limit_bytes=46 * 1024 * 1024),
        cost_estimate=cost,
        name="experts",
    )(place, *xs, w_gate, w_up, w_down)


def add_low(a, b):
    return (a.astype(jnp.float32) + b.astype(jnp.float32)).astype(jnp.bfloat16)


def local(
    resid_in, head_in, gate_in, in_basis, out_basis, step_size, decay_rate, init_state, lengths,
    norm_gain, out_proj, moe_gain, expert_ids, route_weight, placement, w_gate, w_up, w_down,
):
    devices = lax.axis_size("mix")
    depth = devices // 4
    me = lax.axis_index("mix")
    place = me.astype(jnp.int32)[None]
    tokens = head_in.shape[0]
    tok = tokens // devices
    width = head_in.shape[1]
    model = out_proj.shape[1]

    def cross(x, mask):
        return lax.ppermute(x, "mix", [(i, i ^ mask) for i in range(devices)])

    def onward(x, stride=4):
        return lax.ppermute(x, "mix", [(i, (i + stride) % devices) for i in range(devices)])

    proj_y, proj_z = cross(out_proj, 2), cross(out_proj, 4)
    proj_yz = lax.ppermute(
        jnp.where(me % 2 == 0, proj_y, proj_z),
        "mix",
        [(i, i ^ (2 if i % 2 else 4)) for i in range(devices)],
    )
    gains = jnp.take(norm_gain.reshape(devices, width), me ^ jnp.arange(8), axis=0)

    slots = placement.shape[0]
    slot_of = jnp.sum(
        jnp.where(
            expert_ids[:, :, None] == jnp.arange(slots, dtype=jnp.int32), placement[None, None, :], 0
        ),
        axis=2,
    )
    route = jnp.sum(
        jnp.where(
            slot_of[:, :, None] == jnp.arange(slots, dtype=jnp.int32), route_weight[:, :, None], 0.0
        ),
        axis=1,
    )
    route_high = lax.reduce_precision(route, 8, 7)
    table = jnp.concatenate([route_high, route - route_high], axis=1)
    table = jnp.pad(table, ((0, 0), (0, LANES - 2 * slots))).astype(jnp.bfloat16)

    gated = scan_heads(
        head_in, gate_in, in_basis, out_basis, step_size, decay_rate, init_state, lengths,
        place, depth // 2,
    )
    projs = []
    for block in (out_proj, proj_y, proj_z, proj_yz):
        projs += [block, cross(block, 1)]
    acts = [gated[0]] + [cross(gated[mask], mask) for mask in range(1, 8)]
    sums = []
    for half, (start, steps) in enumerate(((0, 1), (1, 3))):
        mixed, squares = project(gains, acts, projs, start, steps, model // 4, half == 1)
        total = mixed[1]
        if half == 1:
            norm = squares[1]
        for dz in range(2, depth // 2):
            total = add_low(onward(total, 8), mixed[dz])
            if half == 1:
                norm = onward(norm, 8) + squares[dz]
        total = onward(total, 8).astype(jnp.float32) + mixed[0].astype(jnp.float32)
        if half == 1:
            norm = (onward(norm, 8) + squares[0])[:, 0:1]
        sums.append(total)
    mixer_sum = jnp.concatenate(sums, axis=1)
    hidden = resid_in.astype(jnp.float32) + mixer_sum * lax.rsqrt(norm / (devices * width) + epsilon)
    normed = (
        hidden * lax.rsqrt(jnp.mean(hidden * hidden, axis=1, keepdims=True) + epsilon) * moe_gain
    ).astype(jnp.bfloat16)
    mine = jnp.concatenate([normed, table], axis=1)

    cap = 2 * tok * expert_ids.shape[1] // slots
    cut = model // 2 + LANES
    sides = (slice(0, cut), slice(cut, model))
    sums = []
    for dz in range(depth):
        if dz > 0:
            mine = onward(mine)
        other = cross(mine, 2) if dz < depth - 1 else onward(other)
        block = [mine, cross(mine, 1), other, cross(other, 1)]
        outs = run_experts(block, w_gate, w_up, w_down, place, cap, slots, 1)
        near_c, far_c = cross(outs[1], 1), cross(outs[3], 1)
        if dz < depth - 1:
            far = cross(add_low(outs[2], far_c), 2)
            sums.append((outs[0], near_c, far))
        else:
            last = []
            for side in sides:
                far = cross(add_low(outs[2][:, side], far_c[:, side]), 2)
                last.append((outs[0][:, side], near_c[:, side], far))

    def add_all(*terms):
        return sum(t.astype(jnp.float32) for t in terms)

    total = add_all(*sums[1]).astype(jnp.bfloat16)
    for dz in range(2, depth - 1):
        total = add_all(onward(total), *sums[dz]).astype(jnp.bfloat16)
    results = []
    for h, side in enumerate(sides):
        part = onward(total[:, side])
        part = add_all(part, *last[h]).astype(jnp.bfloat16)
        part = onward(part)
        results.append(hidden[:, side] + add_all(part, *(term[:, side] for term in sums[0])))
    return jnp.concatenate(results, axis=1).astype(jnp.bfloat16)


def solution(mesh):
    return jax.shard_map(
        local,
        mesh=mesh,
        in_specs=(
            P(("groups", "mix"), None),
            P("groups", "mix"),
            P("groups", "mix"),
            P("groups", None),
            P("groups", None),
            P("mix", "groups"),
            P("mix"),
            P("groups", "mix", None, None),
            P("groups"),
            P(),
            P("mix", None),
            P(),
            P(("groups", "mix"), None),
            P(("groups", "mix"), None),
            P(),
            P("mix", None, None),
            P("mix", None, None),
            P("mix", None, None),
        ),
        out_specs=P(("groups", "mix"), None),
        check_vma=False,
    )
```

```python
import functools

import jax
import jax.numpy as jnp
from jax import lax
from jax.experimental import pallas as pl
from jax.experimental.pallas import tpu as pltpu
from jax.sharding import PartitionSpec as P


epsilon = 1e-05
LANES = 128
NT = (((1,), (1,)), ((), ()))
TN = (((0,), (0,)), ((), ()))


def mm(a, b, dims=(((1,), (0,)), ((), ())), precision=None):
    return lax.dot_general(
        a, b, dims, precision=precision, preferred_element_type=jnp.float32
    )


def scan_kernel(
    lengths, place, rates, step_ref, x_ref, g_ref, b_ref, c_ref, init_ref, *refs, span, chunks
):
    out_refs, (runs, rows, state, src, first_src) = refs[:8], refs[8:]
    heads, tokens = step_ref.shape
    requests, width, _ = init_ref.shape
    tok = out_refs[0].shape[1]
    head_dim = width // heads
    starts = [jnp.int32(0)]
    for r in range(requests - 1):
        starts.append(starts[-1] + lengths[r])

    @pl.when(pl.program_id(0) == 0)
    def _():
        state[...] = jnp.zeros_like(state)
        runs[...] = jnp.zeros_like(runs)
        for h in range(heads):
            runs[h : h + 1, :] = -step_ref[h : h + 1, :] * rates[h]
        run = runs[...]
        lane = lax.broadcasted_iota(jnp.int32, run.shape, 1)
        inner = lane % span
        shift = 1
        while shift < span:
            run = run + jnp.where(inner >= shift, pltpu.roll(run, shift, 1), 0.0)
            shift *= 2
        runs[...] = run
        final = lane - inner + (span - 1)
        before = jnp.zeros_like(run)
        first_last = jnp.zeros_like(lane)
        for start in starts:
            end = start - start % span + span
            inside = jnp.logical_and(lane == start - 1, start % span > 0)
            value = jnp.sum(jnp.where(inside, run, 0.0), axis=1, keepdims=True)
            before = jnp.where(jnp.logical_and(lane >= start, lane < end), value, before)
            first_last = jnp.where(final >= start, start, first_last)
        weight = jnp.exp(run - before)
        ends = [
            jnp.broadcast_to(run[:, at + span - 1 : at + span], (8, span))
            for at in range(0, tokens, span)
        ]
        ends = jnp.concatenate(ends, axis=1)
        last = jnp.where(lane >= first_last, jnp.exp(ends - run), 0.0)
        zeros = jnp.zeros_like(run)
        steps = jnp.concatenate([step_ref[...], zeros[heads:]], axis=0)
        for i, value in enumerate((steps, last, weight)):
            high = value.astype(jnp.bfloat16)
            low = (value - high.astype(jnp.float32)).astype(jnp.bfloat16)
            rows[16 * i : 16 * i + 16, :] = jnp.concatenate([high, low], axis=0)

    spread_row = lax.broadcasted_iota(jnp.int32, (48, 3 * width), 0)
    spread_col = lax.broadcasted_iota(jnp.int32, (48, 3 * width), 1)
    spread = jnp.logical_and(
        spread_row // 16 == spread_col // width, spread_row % 8 == spread_col % width // head_dim
    )
    spread = jnp.where(spread, 1.0, 0.0).astype(jnp.bfloat16)
    row = lax.broadcasted_iota(jnp.int32, (span, span), 0)
    col = lax.broadcasted_iota(jnp.int32, (span, span), 1)
    causal = col <= row
    per_tile = LANES // head_dim
    tile_lane = lax.broadcasted_iota(jnp.int32, (span, LANES), 1) // head_dim
    local_pos = lax.broadcasted_iota(jnp.int32, (span, 1), 0)

    for u in range(chunks):
        chunk = pl.program_id(0) * chunks + u
        c0 = pl.multiple_of(chunk * span, span)
        here = pl.ds(u * span, span)
        run = runs[:, pl.ds(c0, span)]
        pos = local_pos + c0
        first = jnp.zeros_like(pos)
        for start in starts:
            first = jnp.where(pos >= start, start, first)
        spread_all = mm(rows[:, pl.ds(c0, span)], spread, TN)
        weight_wide = spread_all[:, 2 * width :]
        drive = x_ref[here, :].astype(jnp.float32) * spread_all[:, :width]
        drive_low = drive.astype(jnp.bfloat16)
        drive_last = (drive * spread_all[:, width : 2 * width]).astype(jnp.bfloat16)
        basis = b_ref[here, :]
        readout = c_ref[here, :]
        valid = jnp.logical_and(causal, col >= first - c0)
        scores = jnp.where(valid, mm(readout, basis, NT), 0.0)

        src[...] = mm(readout, state[...].astype(jnp.bfloat16))
        first_src[...] = state[...]
        for r, start in enumerate(starts):

            @pl.when(jnp.logical_and(start >= c0, start < c0 + span))
            def _(r=r, start=start):
                init = init_ref[r].T
                mine = mm(readout, init.astype(jnp.bfloat16))
                src[...] = jnp.where(first == start, mine, src[...])
                first_src[...] = init

        run_cols = run.T
        pieces = []
        for tile in range(heads // per_tile):
            drive_tile = drive_low[:, tile * LANES : (tile + 1) * LANES]
            piece = None
            for j in range(per_tile):
                h = tile * per_tile + j
                gap = jnp.minimum(run_cols[:, h : h + 1] - run[h : h + 1, :], 0.0)
                part = mm((jnp.exp(gap) * scores).astype(jnp.bfloat16), drive_tile)
                piece = part if piece is None else jnp.where(tile_lane == j, part, piece)
            pieces.append(piece)
        within = pieces[0] if len(pieces) == 1 else jnp.concatenate(pieces, axis=1)
        output = within + weight_wide * src[...]
        state[...] = mm(basis, drive_last, TN) + weight_wide[span - 1 : span, :] * first_src[...]
        gate = g_ref[here, :].astype(jnp.float32)
        gated = (output * (gate / (1.0 + jnp.exp(-gate)))).astype(jnp.bfloat16)
        even = lax.rem(place[0], 2) == 0
        mine = jnp.where(even, gated[:tok], gated[tok:])
        other = jnp.where(even, gated[tok:], gated[:tok])
        pair = lax.rem(chunk, 4) ^ lax.div(lax.rem(place[0], 8), 2)
        for way in range(4):

            @pl.when(pair == way)
            def _(way=way, mine=mine, other=other):
                out_refs[2 * way][0] = mine
                out_refs[2 * way + 1][0] = other


def scan_heads(head_in, gate_in, in_basis, out_basis, step, rate, init, lengths, place, depth):
    tokens, width = head_in.shape
    heads = step.shape[0]
    requests = lengths.shape[0]
    states = in_basis.shape[1]
    tok = tokens // (8 * depth)
    span = 2 * tok
    chunks = 2
    block = chunks * span
    init = init.reshape(requests, width, states)
    cost = pl.CostEstimate(
        flops=2 * tokens * width * (span * 2 + 3 * states),
        bytes_accessed=6 * tokens * width,
        transcendentals=tokens * span * heads,
    )

    def row_block(i, lengths, place, rates):
        return (i, 0)

    def out_block(i, lengths, place, rates):
        return (lax.rem(lax.div(place[0], 8) - lax.div(i * chunks, 4) + depth, depth), 0, 0)

    return pl.pallas_call(
        functools.partial(scan_kernel, span=span, chunks=chunks),
        out_shape=[jax.ShapeDtypeStruct((depth, tok, width), jnp.bfloat16)] * 8,
        grid_spec=pltpu.PrefetchScalarGridSpec(
            num_scalar_prefetch=3,
            grid=(tokens // block,),
            in_specs=[
                pl.BlockSpec((heads, tokens), lambda i, lengths, place, rates: (0, 0)),
                pl.BlockSpec((block, width), row_block),
                pl.BlockSpec((block, width), row_block),
                pl.BlockSpec((block, states), row_block),
                pl.BlockSpec((block, states), row_block),
                pl.BlockSpec((requests, width, states), lambda i, lengths, place, rates: (0, 0, 0)),
            ],
            out_specs=[pl.BlockSpec((1, tok, width), out_block)] * 8,
            scratch_shapes=[
                pltpu.VMEM((8, tokens), jnp.float32),
                pltpu.VMEM((48, tokens), jnp.bfloat16),
                pltpu.VMEM((states, width), jnp.float32),
                pltpu.VMEM((span, width), jnp.float32),
                pltpu.VMEM((states, width), jnp.float32),
            ],
        ),
        cost_estimate=cost,
        name="scan",
    )(lengths, place, rate, step, head_in, gate_in, in_basis, out_basis, init)


def project_kernel(place, *refs, depth, squared):
    gain_ref, acts, refs = refs[0], refs[1:9], refs[9:]
    weights, refs = refs[:8], refs[8:]
    outs, squares = refs[:depth], refs[depth:]
    _, tok, width = acts[0].shape
    total = None
    for mask, act in enumerate(acts):
        rows = act[...].reshape(depth * tok, width).astype(jnp.float32)
        rows = (rows * gain_ref[pl.ds(place[0] ^ mask, 1), :]).astype(jnp.bfloat16)
        part = mm(rows, weights[mask][...])
        total = part if total is None else total + part
    for dz in range(depth):
        outs[dz][...] = total[dz * tok : (dz + 1) * tok].astype(jnp.bfloat16)
    if squared:

        @pl.when(pl.program_id(0) == 0)
        def _():
            for dz in range(depth):
                wide = [act[dz].astype(jnp.float32) for act in acts]
                summed = sum(jnp.sum(w * w, axis=1, keepdims=True) for w in wide)
                squares[dz][...] = jnp.broadcast_to(summed, (tok, LANES))


def project(place, gains, acts, weights, start, steps, columns, squared):
    depth, tok, width = acts[0].shape
    part = steps * columns
    cost = pl.CostEstimate(
        flops=16 * depth * tok * width * part,
        bytes_accessed=2 * (8 * width * part + depth * tok * (part + 8 * width)),
        transcendentals=0,
    )
    out_shape = [jax.ShapeDtypeStruct((tok, columns * steps), jnp.bfloat16)] * depth
    out_specs = [pl.BlockSpec((tok, columns), lambda i, place: (0, i))] * depth
    if squared:
        out_shape += [jax.ShapeDtypeStruct((tok, LANES), jnp.float32)] * depth
        out_specs += [pl.BlockSpec((tok, LANES), lambda i, place: (0, 0))] * depth
    out = pl.pallas_call(
        functools.partial(project_kernel, depth=depth, squared=squared),
        out_shape=out_shape,
        grid_spec=pltpu.PrefetchScalarGridSpec(
            num_scalar_prefetch=1,
            grid=(steps,),
            in_specs=[pl.BlockSpec(gains.shape, lambda i, place: (0, 0))]
            + [pl.BlockSpec((depth, tok, width), lambda i, place: (0, 0, 0))] * 8
            + [pl.BlockSpec((width, columns), lambda i, place: (0, start + i))] * 8,
            out_specs=out_specs,
        ),
        compiler_params=pltpu.CompilerParams(vmem_limit_bytes=20 * 1024 * 1024),
        cost_estimate=cost,
        name="project",
    )(place, gains, *acts, *weights)
    return out[:depth], out[depth:]


def expert_kernel(place, owner_ref, *refs, blocks, cap):
    x_refs = refs[:blocks]
    gate_ref, up_ref, down_ref = refs[blocks : blocks + 3]
    outs = refs[blocks + 3 : 2 * blocks + 3]
    rows, total, combine, results = refs[2 * blocks + 3 :]
    expert, part = pl.program_id(0), pl.program_id(1)
    tok, model = outs[0].shape
    count = rows.shape[0]
    wide = count * cap

    @pl.when(jnp.logical_and(expert == 0, part == 0))
    def _():
        here = place[0] * count + lax.broadcasted_iota(jnp.int32, (LANES, wide), 1) // cap
        pick = jnp.where(owner_ref[...] == here, 1.0, 0.0).astype(jnp.bfloat16)
        below = lax.broadcasted_iota(jnp.int32, (tok, tok), 0)
        across = lax.broadcasted_iota(jnp.int32, (tok, tok), 1)
        earlier = jnp.where(across < below, 1.0, 0.0).astype(jnp.bfloat16)
        slot = (lax.broadcasted_iota(jnp.int32, (tok, wide), 1) % cap).astype(jnp.float32)
        for b in range(blocks):
            weight = mm(x_refs[b][:, model : model + LANES], pick)
            chosen = weight > 0.0
            rank = mm(earlier, jnp.where(chosen, 1.0, 0.0).astype(jnp.bfloat16))
            match = jnp.logical_and(chosen, rank == slot)
            select = jnp.where(match, 1.0, 0.0).astype(jnp.bfloat16)
            picked = mm(select, x_refs[b][:, :model], TN).astype(jnp.bfloat16)
            for e in range(count):
                rows[e, b * cap : (b + 1) * cap, :] = picked[e * cap : (e + 1) * cap]
            weight = jnp.where(match, weight, 0.0)
            high = weight.astype(jnp.bfloat16)
            low = (weight - high.astype(jnp.float32)).astype(jnp.bfloat16)
            combine[b] = jnp.concatenate([high, low], axis=1)

    x = rows[expert]
    gate = mm(x, gate_ref[0])
    up = mm(x, up_ref[0])
    act = (gate / (1.0 + jnp.exp(-gate)) * up).astype(jnp.bfloat16)
    down = mm(act, down_ref[0])

    @pl.when(part == 0)
    def _():
        total[...] = down

    @pl.when(part > 0)
    def _():
        total[...] += down

    @pl.when(part == pl.num_programs(1) - 1)
    def _():
        for b in range(blocks):
            value = total[b * cap : (b + 1) * cap, :].astype(jnp.bfloat16)
            results[b, pl.ds(pl.multiple_of(expert * cap, cap), cap), :] = value
            results[b, pl.ds(pl.multiple_of(wide + expert * cap, cap), cap), :] = value

    @pl.when(jnp.logical_and(expert == count - 1, part == pl.num_programs(1) - 1))
    def _():
        for b in range(blocks):
            outs[b][...] = mm(combine[b], results[b]).astype(jnp.bfloat16)


def run_experts(xs, w_gate, w_up, w_down, place, owner, cap, parts):
    blocks = len(xs)
    tok, extended = xs[0].shape
    count, model, hidden = w_gate.shape
    tile = hidden // parts
    cost = pl.CostEstimate(
        flops=6 * count * blocks * cap * model * hidden,
        bytes_accessed=6 * count * model * hidden + 4 * blocks * tok * model,
        transcendentals=count * blocks * cap * hidden,
    )
    return pl.pallas_call(
        functools.partial(expert_kernel, blocks=blocks, cap=cap),
        out_shape=[jax.ShapeDtypeStruct((tok, model), jnp.bfloat16)] * blocks,
        grid_spec=pltpu.PrefetchScalarGridSpec(
            num_scalar_prefetch=1,
            grid=(count, parts),
            in_specs=[pl.BlockSpec(owner.shape, lambda e, f, place: (0, 0))]
            + [pl.BlockSpec((tok, extended), lambda e, f, place: (0, 0))] * blocks
            + [
                pl.BlockSpec((1, model, tile), lambda e, f, place: (e, 0, f)),
                pl.BlockSpec((1, model, tile), lambda e, f, place: (e, 0, f)),
                pl.BlockSpec((1, tile, model), lambda e, f, place: (e, f, 0)),
            ],
            out_specs=[pl.BlockSpec((tok, model), lambda e, f, place: (0, 0))] * blocks,
            scratch_shapes=[
                pltpu.VMEM((count, blocks * cap, model), jnp.bfloat16),
                pltpu.VMEM((blocks * cap, model), jnp.float32),
                pltpu.VMEM((blocks, tok, 2 * count * cap), jnp.bfloat16),
                pltpu.VMEM((blocks, 2 * count * cap, model), jnp.bfloat16),
            ],
        ),
        compiler_params=pltpu.CompilerParams(vmem_limit_bytes=40 * 1024 * 1024),
        cost_estimate=cost,
        name="experts",
    )(place, owner, *xs, w_gate, w_up, w_down)


def add_low(a, b):
    return (a.astype(jnp.float32) + b.astype(jnp.float32)).astype(jnp.bfloat16)


def local(
    resid_in, head_in, gate_in, in_basis, out_basis, step_size, decay_rate, init_state, lengths,
    norm_gain, out_proj, moe_gain, expert_ids, route_weight, placement, w_gate, w_up, w_down,
):
    devices = lax.axis_size("mix")
    depth = devices // 4
    me = lax.axis_index("mix")
    place = me.astype(jnp.int32)[None]
    tokens = head_in.shape[0]
    tok = tokens // devices
    width = head_in.shape[1]
    model = out_proj.shape[1]

    def cross(x, mask):
        return lax.ppermute(x, "mix", [(i, i ^ mask) for i in range(devices)])

    def onward(x, stride=4):
        return lax.ppermute(x, "mix", [(i, (i + stride) % devices) for i in range(devices)])

    proj_y, proj_z = cross(out_proj, 2), cross(out_proj, 4)
    proj_yz = lax.ppermute(
        jnp.where(me % 2 == 0, proj_y, proj_z),
        "mix",
        [(i, i ^ (2 if i % 2 else 4)) for i in range(devices)],
    )
    gains = norm_gain.reshape(devices, width)

    slots = placement.shape[0]
    column = lax.broadcasted_iota(jnp.int32, (tok, LANES), 1)
    route = jnp.zeros((tok, LANES), jnp.float32)
    for k in range(expert_ids.shape[1]):
        named = expert_ids[:, k : k + 1] == column % slots
        route = route + jnp.where(named, route_weight[:, k : k + 1], 0.0)
    high = lax.reduce_precision(route, 8, 7)
    table = jnp.where(column < slots, high, jnp.where(column < 2 * slots, route - high, 0.0))
    table = table.astype(jnp.bfloat16)
    owner = jnp.concatenate([placement, placement])
    owner = jnp.pad(owner, (0, LANES - 2 * slots), constant_values=-1)[:, None]

    gated = scan_heads(
        head_in, gate_in, in_basis, out_basis, step_size, decay_rate, init_state, lengths,
        place, depth // 2,
    )
    projs = []
    for block in (out_proj, proj_y, proj_z, proj_yz):
        projs += [block, cross(block, 1)]
    acts = [gated[0]] + [cross(gated[mask], mask) for mask in range(1, 8)]
    sums = []
    for half, (start, steps) in enumerate(((0, 2), (2, 2))):
        mixed, squares = project(place, gains, acts, projs, start, steps, model // 4, half == 1)
        total = mixed[1]
        if half == 1:
            norm = squares[1]
        for dz in range(2, depth // 2):
            total = add_low(onward(total, 8), mixed[dz])
            if half == 1:
                norm = onward(norm, 8) + squares[dz]
        total = onward(total, 8).astype(jnp.float32) + mixed[0].astype(jnp.float32)
        if half == 1:
            norm = (onward(norm, 8) + squares[0])[:, 0:1]
        sums.append(total)
    mixer_sum = jnp.concatenate(sums, axis=1)
    hidden = resid_in.astype(jnp.float32) + mixer_sum * lax.rsqrt(norm / (devices * width) + epsilon)
    normed = (
        hidden * lax.rsqrt(jnp.mean(hidden * hidden, axis=1, keepdims=True) + epsilon) * moe_gain
    ).astype(jnp.bfloat16)
    mine = jnp.concatenate([normed, table], axis=1)

    cap = 2 * tok * expert_ids.shape[1] // slots
    cut = model // 2 + LANES
    sides = (slice(0, cut), slice(cut, model))
    sums = []
    for dz in range(depth):
        if dz > 0:
            mine = onward(mine)
        other = cross(mine, 2) if dz < depth - 1 else onward(other)
        block = [mine, cross(mine, 1), other, cross(other, 1)]
        outs = run_experts(block, w_gate, w_up, w_down, place, owner, cap, 1)
        near_c, far_c = cross(outs[1], 1), cross(outs[3], 1)
        if 0 < dz < depth - 1:
            far = cross(add_low(outs[2], far_c), 2)
            sums.append((outs[0], near_c, far))
        else:
            parts = []
            for side in sides:
                far = cross(add_low(outs[2][:, side], far_c[:, side]), 2)
                parts.append((outs[0][:, side], near_c[:, side], far))
            sums.append(parts)

    def add_all(*terms):
        return sum(t.astype(jnp.float32) for t in terms)

    total = add_all(*sums[1]).astype(jnp.bfloat16)
    for dz in range(2, depth - 1):
        total = add_all(onward(total), *sums[dz]).astype(jnp.bfloat16)
    results = []
    for h, side in enumerate(sides):
        part = onward(total[:, side])
        part = add_all(part, *sums[-1][h]).astype(jnp.bfloat16)
        part = onward(part)
        results.append(hidden[:, side] + add_all(part, *sums[0][h]))
    return jnp.concatenate(results, axis=1).astype(jnp.bfloat16)


def solution(mesh):
    return jax.shard_map(
        local,
        mesh=mesh,
        in_specs=(
            P(("groups", "mix"), None),
            P("groups", "mix"),
            P("groups", "mix"),
            P("groups", None),
            P("groups", None),
            P("mix", "groups"),
            P("mix"),
            P("groups", "mix", None, None),
            P("groups"),
            P(),
            P("mix", None),
            P(),
            P(("groups", "mix"), None),
            P(("groups", "mix"), None),
            P(),
            P("mix", None, None),
            P("mix", None, None),
            P("mix", None, None),
        ),
        out_specs=P(("groups", "mix"), None),
        check_vma=False,
    )
```

```python
import functools

import jax
import jax.numpy as jnp
from jax import lax
from jax.experimental import pallas as pl
from jax.experimental.pallas import tpu as pltpu
from jax.sharding import PartitionSpec as P


epsilon = 1e-05
LANES = 128
NT = (((1,), (1,)), ((), ()))
TN = (((0,), (0,)), ((), ()))


def mm(a, b, dims=(((1,), (0,)), ((), ())), precision=None):
    return lax.dot_general(
        a, b, dims, precision=precision, preferred_element_type=jnp.float32
    )


def scan_kernel(
    lengths, place, rates, step_ref, x_ref, g_ref, b_ref, c_ref, init_ref, *refs, span, chunks
):
    out_refs, (runs, rows, state, src, first_src) = refs[:8], refs[8:]
    heads, tokens = step_ref.shape
    requests, width, _ = init_ref.shape
    tok = out_refs[0].shape[1]
    head_dim = width // heads
    starts = [jnp.int32(0)]
    for r in range(requests - 1):
        starts.append(starts[-1] + lengths[r])

    @pl.when(pl.program_id(0) == 0)
    def _():
        state[...] = jnp.zeros_like(state)
        runs[...] = jnp.zeros_like(runs)
        for h in range(heads):
            runs[h : h + 1, :] = -step_ref[h : h + 1, :] * rates[h]
        run = runs[...]
        lane = lax.broadcasted_iota(jnp.int32, run.shape, 1)
        inner = lane % span
        shift = 1
        while shift < span:
            run = run + jnp.where(inner >= shift, pltpu.roll(run, shift, 1), 0.0)
            shift *= 2
        runs[...] = run
        final = lane - inner + (span - 1)
        before = jnp.zeros_like(run)
        first_last = jnp.zeros_like(lane)
        for start in starts:
            end = start - start % span + span
            inside = jnp.logical_and(lane == start - 1, start % span > 0)
            value = jnp.sum(jnp.where(inside, run, 0.0), axis=1, keepdims=True)
            before = jnp.where(jnp.logical_and(lane >= start, lane < end), value, before)
            first_last = jnp.where(final >= start, start, first_last)
        weight = jnp.exp(run - before)
        ends = [
            jnp.broadcast_to(run[:, at + span - 1 : at + span], (8, span))
            for at in range(0, tokens, span)
        ]
        ends = jnp.concatenate(ends, axis=1)
        last = jnp.where(lane >= first_last, jnp.exp(ends - run), 0.0)
        zeros = jnp.zeros_like(run)
        steps = jnp.concatenate([step_ref[...], zeros[heads:]], axis=0)
        for i, value in enumerate((steps, last, weight)):
            high = value.astype(jnp.bfloat16)
            low = (value - high.astype(jnp.float32)).astype(jnp.bfloat16)
            rows[16 * i : 16 * i + 16, :] = jnp.concatenate([high, low], axis=0)

    spread_row = lax.broadcasted_iota(jnp.int32, (48, 3 * width), 0)
    spread_col = lax.broadcasted_iota(jnp.int32, (48, 3 * width), 1)
    spread = jnp.logical_and(
        spread_row // 16 == spread_col // width, spread_row % 8 == spread_col % width // head_dim
    )
    spread = jnp.where(spread, 1.0, 0.0).astype(jnp.bfloat16)
    row = lax.broadcasted_iota(jnp.int32, (span, span), 0)
    col = lax.broadcasted_iota(jnp.int32, (span, span), 1)
    causal = col <= row
    per_tile = LANES // head_dim
    tile_lane = lax.broadcasted_iota(jnp.int32, (span, LANES), 1) // head_dim
    local_pos = lax.broadcasted_iota(jnp.int32, (span, 1), 0)

    for u in range(chunks):
        chunk = pl.program_id(0) * chunks + u
        c0 = pl.multiple_of(chunk * span, span)
        here = pl.ds(u * span, span)
        run = runs[:, pl.ds(c0, span)]
        pos = local_pos + c0
        first = jnp.zeros_like(pos)
        for start in starts:
            first = jnp.where(pos >= start, start, first)
        spread_all = mm(rows[:, pl.ds(c0, span)], spread, TN)
        weight_wide = spread_all[:, 2 * width :]
        drive = x_ref[here, :].astype(jnp.float32) * spread_all[:, :width]
        drive_low = drive.astype(jnp.bfloat16)
        drive_last = (drive * spread_all[:, width : 2 * width]).astype(jnp.bfloat16)
        basis = b_ref[here, :]
        readout = c_ref[here, :]
        valid = jnp.logical_and(causal, col >= first - c0)
        scores = jnp.where(valid, mm(readout, basis, NT), 0.0)

        src[...] = mm(readout, state[...].astype(jnp.bfloat16))
        first_src[...] = state[...]
        for r, start in enumerate(starts):

            @pl.when(jnp.logical_and(start >= c0, start < c0 + span))
            def _(r=r, start=start):
                init = init_ref[r].T
                mine = mm(readout, init.astype(jnp.bfloat16))
                src[...] = jnp.where(first == start, mine, src[...])
                first_src[...] = init

        run_cols = run.T
        pieces = []
        for tile in range(heads // per_tile):
            drive_tile = drive_low[:, tile * LANES : (tile + 1) * LANES]
            piece = None
            for j in range(per_tile):
                h = tile * per_tile + j
                gap = jnp.minimum(run_cols[:, h : h + 1] - run[h : h + 1, :], 0.0)
                part = mm((jnp.exp(gap) * scores).astype(jnp.bfloat16), drive_tile)
                piece = part if piece is None else jnp.where(tile_lane == j, part, piece)
            pieces.append(piece)
        within = pieces[0] if len(pieces) == 1 else jnp.concatenate(pieces, axis=1)
        output = within + weight_wide * src[...]
        state[...] = mm(basis, drive_last, TN) + weight_wide[span - 1 : span, :] * first_src[...]
        gate = g_ref[here, :].astype(jnp.float32)
        gated = (output * (gate / (1.0 + jnp.exp(-gate)))).astype(jnp.bfloat16)
        even = lax.rem(place[0], 2) == 0
        mine = jnp.where(even, gated[:tok], gated[tok:])
        other = jnp.where(even, gated[tok:], gated[:tok])
        pair = lax.rem(chunk, 4) ^ lax.div(lax.rem(place[0], 8), 2)
        for way in range(4):

            @pl.when(pair == way)
            def _(way=way, mine=mine, other=other):
                out_refs[2 * way][0] = mine
                out_refs[2 * way + 1][0] = other


def scan_heads(head_in, gate_in, in_basis, out_basis, step, rate, init, lengths, place, depth):
    tokens, width = head_in.shape
    heads = step.shape[0]
    requests = lengths.shape[0]
    states = in_basis.shape[1]
    tok = tokens // (8 * depth)
    span = 2 * tok
    chunks = 2
    block = chunks * span
    init = init.reshape(requests, width, states)
    cost = pl.CostEstimate(
        flops=2 * tokens * width * (span * 2 + 3 * states),
        bytes_accessed=6 * tokens * width,
        transcendentals=tokens * span * heads,
    )

    def row_block(i, lengths, place, rates):
        return (i, 0)

    def out_block(i, lengths, place, rates):
        return (lax.rem(lax.div(place[0], 8) - lax.div(i * chunks, 4) + depth, depth), 0, 0)

    return pl.pallas_call(
        functools.partial(scan_kernel, span=span, chunks=chunks),
        out_shape=[jax.ShapeDtypeStruct((depth, tok, width), jnp.bfloat16)] * 8,
        grid_spec=pltpu.PrefetchScalarGridSpec(
            num_scalar_prefetch=3,
            grid=(tokens // block,),
            in_specs=[
                pl.BlockSpec((heads, tokens), lambda i, lengths, place, rates: (0, 0)),
                pl.BlockSpec((block, width), row_block),
                pl.BlockSpec((block, width), row_block),
                pl.BlockSpec((block, states), row_block),
                pl.BlockSpec((block, states), row_block),
                pl.BlockSpec((requests, width, states), lambda i, lengths, place, rates: (0, 0, 0)),
            ],
            out_specs=[pl.BlockSpec((1, tok, width), out_block)] * 8,
            scratch_shapes=[
                pltpu.VMEM((8, tokens), jnp.float32),
                pltpu.VMEM((48, tokens), jnp.bfloat16),
                pltpu.VMEM((states, width), jnp.float32),
                pltpu.VMEM((span, width), jnp.float32),
                pltpu.VMEM((states, width), jnp.float32),
            ],
        ),
        cost_estimate=cost,
        name="scan",
    )(lengths, place, rate, step, head_in, gate_in, in_basis, out_basis, init)


def project_kernel(place, *refs, depth, squared):
    gain_ref, acts, refs = refs[0], refs[1:9], refs[9:]
    weights, refs = refs[:8], refs[8:]
    outs, squares = refs[:depth], refs[depth:]
    _, tok, width = acts[0].shape
    total = None
    for mask, act in enumerate(acts):
        rows = act[...].reshape(depth * tok, width).astype(jnp.float32)
        rows = (rows * gain_ref[pl.ds(place[0] ^ mask, 1), :]).astype(jnp.bfloat16)
        part = mm(rows, weights[mask][...])
        total = part if total is None else total + part
    for dz in range(depth):
        outs[dz][...] = total[dz * tok : (dz + 1) * tok].astype(jnp.bfloat16)
    if squared:

        @pl.when(pl.program_id(0) == 0)
        def _():
            for dz in range(depth):
                wide = [act[dz].astype(jnp.float32) for act in acts]
                summed = sum(jnp.sum(w * w, axis=1, keepdims=True) for w in wide)
                squares[dz][...] = jnp.broadcast_to(summed, (tok, LANES))


def project(place, gains, acts, weights, start, steps, columns, squared):
    depth, tok, width = acts[0].shape
    model = weights[0].shape[1]
    part = steps * columns
    cost = pl.CostEstimate(
        flops=16 * depth * tok * width * part,
        bytes_accessed=2 * (8 * width * part + depth * tok * (part + 8 * width)),
        transcendentals=0,
    )
    out_shape = [jax.ShapeDtypeStruct((tok, columns * steps), jnp.bfloat16)] * depth
    out_specs = [pl.BlockSpec((tok, columns), lambda i, place: (0, i))] * depth
    if squared:
        out_shape += [jax.ShapeDtypeStruct((tok, LANES), jnp.float32)] * depth
        out_specs += [pl.BlockSpec((tok, LANES), lambda i, place: (0, 0))] * depth
    out = pl.pallas_call(
        functools.partial(project_kernel, depth=depth, squared=squared),
        out_shape=out_shape,
        grid_spec=pltpu.PrefetchScalarGridSpec(
            num_scalar_prefetch=1,
            grid=(steps,),
            in_specs=[pl.BlockSpec(gains.shape, lambda i, place: (0, 0))]
            + [pl.BlockSpec((depth, tok, width), lambda i, place: (0, 0, 0))] * 8
            + [
                pl.BlockSpec(
                    (width, columns),
                    functools.partial(
                        lambda first, i, place: (0, first + i), start if w.shape[1] == model else 0
                    ),
                )
                for w in weights
            ],
            out_specs=out_specs,
        ),
        compiler_params=pltpu.CompilerParams(vmem_limit_bytes=20 * 1024 * 1024),
        cost_estimate=cost,
        name="project",
    )(place, gains, *acts, *weights)
    return out[:depth], out[depth:]


def expert_kernel(place, owner_ref, *refs, blocks, cap):
    x_refs = refs[:blocks]
    gate_ref, up_ref, down_ref = refs[blocks : blocks + 3]
    outs = refs[blocks + 3 : 2 * blocks + 3]
    rows, total, combine, results = refs[2 * blocks + 3 :]
    expert, part = pl.program_id(0), pl.program_id(1)
    tok, model = outs[0].shape
    count = rows.shape[0]
    wide = count * cap

    @pl.when(jnp.logical_and(expert == 0, part == 0))
    def _():
        here = place[0] * count + lax.broadcasted_iota(jnp.int32, (LANES, wide), 1) // cap
        pick = jnp.where(owner_ref[...] == here, 1.0, 0.0).astype(jnp.bfloat16)
        below = lax.broadcasted_iota(jnp.int32, (tok, tok), 0)
        across = lax.broadcasted_iota(jnp.int32, (tok, tok), 1)
        earlier = jnp.where(across < below, 1.0, 0.0).astype(jnp.bfloat16)
        slot = (lax.broadcasted_iota(jnp.int32, (tok, wide), 1) % cap).astype(jnp.float32)
        for b in range(blocks):
            weight = mm(x_refs[b][:, model : model + LANES], pick)
            chosen = weight > 0.0
            rank = mm(earlier, jnp.where(chosen, 1.0, 0.0).astype(jnp.bfloat16))
            match = jnp.logical_and(chosen, rank == slot)
            select = jnp.where(match, 1.0, 0.0).astype(jnp.bfloat16)
            picked = mm(select, x_refs[b][:, :model], TN).astype(jnp.bfloat16)
            for e in range(count):
                rows[e, b * cap : (b + 1) * cap, :] = picked[e * cap : (e + 1) * cap]
            weight = jnp.where(match, weight, 0.0)
            high = weight.astype(jnp.bfloat16)
            low = (weight - high.astype(jnp.float32)).astype(jnp.bfloat16)
            combine[b] = jnp.concatenate([high, low], axis=1)

    x = rows[expert]
    gate = mm(x, gate_ref[0])
    up = mm(x, up_ref[0])
    act = (gate / (1.0 + jnp.exp(-gate)) * up).astype(jnp.bfloat16)
    down = mm(act, down_ref[0])

    @pl.when(part == 0)
    def _():
        total[...] = down

    @pl.when(part > 0)
    def _():
        total[...] += down

    @pl.when(part == pl.num_programs(1) - 1)
    def _():
        for b in range(blocks):
            value = total[b * cap : (b + 1) * cap, :].astype(jnp.bfloat16)
            results[b, pl.ds(pl.multiple_of(expert * cap, cap), cap), :] = value
            results[b, pl.ds(pl.multiple_of(wide + expert * cap, cap), cap), :] = value

    @pl.when(jnp.logical_and(expert == count - 1, part == pl.num_programs(1) - 1))
    def _():
        for b in range(blocks):
            outs[b][...] = mm(combine[b], results[b]).astype(jnp.bfloat16)


def run_experts(xs, w_gate, w_up, w_down, place, owner, cap, parts):
    blocks = len(xs)
    tok, extended = xs[0].shape
    count, model, hidden = w_gate.shape
    tile = hidden // parts
    cost = pl.CostEstimate(
        flops=6 * count * blocks * cap * model * hidden,
        bytes_accessed=6 * count * model * hidden + 4 * blocks * tok * model,
        transcendentals=count * blocks * cap * hidden,
    )
    return pl.pallas_call(
        functools.partial(expert_kernel, blocks=blocks, cap=cap),
        out_shape=[jax.ShapeDtypeStruct((tok, model), jnp.bfloat16)] * blocks,
        grid_spec=pltpu.PrefetchScalarGridSpec(
            num_scalar_prefetch=1,
            grid=(count, parts),
            in_specs=[pl.BlockSpec(owner.shape, lambda e, f, place: (0, 0))]
            + [pl.BlockSpec((tok, extended), lambda e, f, place: (0, 0))] * blocks
            + [
                pl.BlockSpec((1, model, tile), lambda e, f, place: (e, 0, f)),
                pl.BlockSpec((1, model, tile), lambda e, f, place: (e, 0, f)),
                pl.BlockSpec((1, tile, model), lambda e, f, place: (e, f, 0)),
            ],
            out_specs=[pl.BlockSpec((tok, model), lambda e, f, place: (0, 0))] * blocks,
            scratch_shapes=[
                pltpu.VMEM((count, blocks * cap, model), jnp.bfloat16),
                pltpu.VMEM((blocks * cap, model), jnp.float32),
                pltpu.VMEM((blocks, tok, 2 * count * cap), jnp.bfloat16),
                pltpu.VMEM((blocks, 2 * count * cap, model), jnp.bfloat16),
            ],
        ),
        compiler_params=pltpu.CompilerParams(vmem_limit_bytes=40 * 1024 * 1024),
        cost_estimate=cost,
        name="experts",
    )(place, owner, *xs, w_gate, w_up, w_down)


def add_low(a, b):
    return (a.astype(jnp.float32) + b.astype(jnp.float32)).astype(jnp.bfloat16)


def local(
    resid_in, head_in, gate_in, in_basis, out_basis, step_size, decay_rate, init_state, lengths,
    norm_gain, out_proj, moe_gain, expert_ids, route_weight, placement, w_gate, w_up, w_down,
):
    devices = lax.axis_size("mix")
    depth = devices // 4
    me = lax.axis_index("mix")
    place = me.astype(jnp.int32)[None]
    tokens = head_in.shape[0]
    tok = tokens // devices
    width = head_in.shape[1]
    model = out_proj.shape[1]

    def cross(x, mask):
        return lax.ppermute(x, "mix", [(i, i ^ mask) for i in range(devices)])

    def onward(x, stride=4):
        return lax.ppermute(x, "mix", [(i, (i + stride) % devices) for i in range(devices)])

    proj_y, proj_z = cross(out_proj, 2), cross(out_proj, 4)
    proj_yz = jnp.where(me % 2 == 0, proj_y, proj_z)
    diagonal = []
    for half in range(2):
        diagonal.append(
            lax.ppermute(
                proj_yz[:, half * model // 2 : (half + 1) * model // 2],
                "mix",
                [(i, i ^ (2 if i % 2 else 4)) for i in range(devices)],
            )
        )
    gains = norm_gain.reshape(devices, width)

    slots = placement.shape[0]
    column = lax.broadcasted_iota(jnp.int32, (tok, LANES), 1)
    route = jnp.zeros((tok, LANES), jnp.float32)
    for k in range(expert_ids.shape[1]):
        named = expert_ids[:, k : k + 1] == column % slots
        route = route + jnp.where(named, route_weight[:, k : k + 1], 0.0)
    high = lax.reduce_precision(route, 8, 7)
    table = jnp.where(column < slots, high, jnp.where(column < 2 * slots, route - high, 0.0))
    table = table.astype(jnp.bfloat16)
    owner = jnp.concatenate([placement, placement])
    owner = jnp.pad(owner, (0, LANES - 2 * slots), constant_values=-1)[:, None]

    gated = scan_heads(
        head_in, gate_in, in_basis, out_basis, step_size, decay_rate, init_state, lengths,
        place, depth // 2,
    )
    projs = []
    for block in (out_proj, proj_y, proj_z):
        projs += [block, cross(block, 1)]
    acts = [gated[0]] + [cross(gated[mask], mask) for mask in range(1, 8)]
    sums = []
    for half, (start, steps) in enumerate(((0, 2), (2, 2))):
        across = [diagonal[half], cross(diagonal[half], 1)]
        mixed, squares = project(place, gains, acts, projs + across, start, steps, model // 4, half == 1)
        total = mixed[1]
        if half == 1:
            norm = squares[1]
        for dz in range(2, depth // 2):
            total = add_low(onward(total, 8), mixed[dz])
            if half == 1:
                norm = onward(norm, 8) + squares[dz]
        total = onward(total, 8).astype(jnp.float32) + mixed[0].astype(jnp.float32)
        if half == 1:
            norm = (onward(norm, 8) + squares[0])[:, 0:1]
        sums.append(total)
    mixer_sum = jnp.concatenate(sums, axis=1)
    hidden = resid_in.astype(jnp.float32) + mixer_sum * lax.rsqrt(norm / (devices * width) + epsilon)
    normed = (
        hidden * lax.rsqrt(jnp.mean(hidden * hidden, axis=1, keepdims=True) + epsilon) * moe_gain
    ).astype(jnp.bfloat16)
    mine = jnp.concatenate([normed, table], axis=1)

    cap = 2 * tok * expert_ids.shape[1] // slots
    cut = model // 2 + LANES
    sides = (slice(0, cut), slice(cut, model))
    sums = []
    for dz in range(depth):
        if dz > 0:
            mine = onward(mine)
        other = cross(mine, 2) if dz < depth - 1 else onward(other)
        block = [mine, cross(mine, 1), other, cross(other, 1)]
        outs = run_experts(block, w_gate, w_up, w_down, place, owner, cap, 1)
        near_c, far_c = cross(outs[1], 1), cross(outs[3], 1)
        if 0 < dz < depth - 1:
            far = cross(add_low(outs[2], far_c), 2)
            sums.append((outs[0], near_c, far))
        else:
            parts = []
            for side in sides:
                far = cross(add_low(outs[2][:, side], far_c[:, side]), 2)
                parts.append((outs[0][:, side], near_c[:, side], far))
            sums.append(parts)

    def add_all(*terms):
        return sum(t.astype(jnp.float32) for t in terms)

    total = add_all(*sums[1]).astype(jnp.bfloat16)
    for dz in range(2, depth - 1):
        total = add_all(onward(total), *sums[dz]).astype(jnp.bfloat16)
    results = []
    for h, side in enumerate(sides):
        part = onward(total[:, side])
        part = add_all(part, *sums[-1][h]).astype(jnp.bfloat16)
        part = onward(part)
        results.append(hidden[:, side] + add_all(part, *sums[0][h]))
    return jnp.concatenate(results, axis=1).astype(jnp.bfloat16)


def solution(mesh):
    return jax.shard_map(
        local,
        mesh=mesh,
        in_specs=(
            P(("groups", "mix"), None),
            P("groups", "mix"),
            P("groups", "mix"),
            P("groups", None),
            P("groups", None),
            P("mix", "groups"),
            P("mix"),
            P("groups", "mix", None, None),
            P("groups"),
            P(),
            P("mix", None),
            P(),
            P(("groups", "mix"), None),
            P(("groups", "mix"), None),
            P(),
            P("mix", None, None),
            P("mix", None, None),
            P("mix", None, None),
        ),
        out_specs=P(("groups", "mix"), None),
        check_vma=False,
    )
```
